128 devices in a mesh: row: 4 (over x), col: 32 (over y, z, core).
Axes of the slice: x: 4, y: 4, z: 4, core: 2. Of those that a mesh axis runs over, the one named last changes fastest.
Arguments:
- factor: float32 [16384, 16384], P('row', 'col'), may hold values from -1 to 2, as said below
- adjoint: float32 [16384, 16384], P('row', 'col'), may hold values from -6 to 6
Outputs:
- panel_adjoint: float32 [16384, 512], P('row')
The draws below stay inside these ranges and needn't reach their ends.
Inputs may be any that keep to these rules, and one draw needn't show every extreme that they name: In global order, every diagonal block of factor is lower triangular with diagonal entries from 1 to 2.
All inputs are finite; a program needn't handle non-finite values.
Results may differ from the reference program's by a relative error of at most 0.0003.
Values sent between devices are 32-bit elements; how exact they have to be, the bound alone decides.
A program may use at most 192 MiB of HBM per device.

```python
import math
import jax
import jax.numpy as jnp
from jax import lax

NB = 256
BC = 2
ROWS_GRID = 4
COLS_GRID = 32
MB = 64
BR = 16
N = 16384


def draw_factor(key, part):
    normal_key, unit_key = jax.random.split(key)
    row_ids = jnp.arange(N, dtype=jnp.int32)
    block_of = row_ids // NB
    offset = row_ids % NB
    global_row = (block_of % BR * ROWS_GRID + block_of // BR) * NB + offset
    global_col = (block_of % BC * COLS_GRID + block_of // BC) * NB + offset
    spread = jnp.clip(jax.random.normal(normal_key, (N, N), jnp.float32), -6.0, 6.0)
    spread = spread * (1.0 / math.sqrt(N))
    unit = jax.random.uniform(unit_key, (N, N), jnp.float32)
    row_grid = global_row[:, None]
    col_grid = global_col[None, :]
    same_block = row_grid // NB == col_grid // NB
    inside = jnp.where(row_grid == col_grid, 1.0 + unit, jnp.where(row_grid > col_grid, (2.0 * unit - 1.0) * (0.9 / NB), 0.0))
    return jnp.where(same_block, inside, spread)


def block_levels(key, dims, cuts, smallest, high):
    factor_of, own = 1.0, jax.random.fold_in(key, 6)
    for axis_at, shards_of in cuts:
        heights = jnp.exp(jax.random.uniform(jax.random.fold_in(own, axis_at), (shards_of,), jnp.float32, smallest / len(cuts), high / len(cuts)))
        factor_of = factor_of * jnp.repeat(heights, dims[axis_at] // shards_of).reshape([-1 if axis == axis_at else 1 for axis in range(len(dims))])
    return factor_of


def scatter_about(rng, dims, scale, limit, cuts=(), held_as=jnp.bfloat16):
    factor_of = block_levels(rng, dims, cuts, -0.22, 0.18) if cuts else 1.0
    values = jax.random.normal(rng, dims, jnp.float32) * scale * factor_of
    return jnp.minimum(jnp.maximum(values, -limit), limit).astype(held_as)


def setup_inputs(seed: int = 0) -> dict:
    seeds = jax.random.split(jax.random.key(seed), 3)
    return {
        "factor": draw_factor(jax.random.fold_in(seeds[2], 71), 0),
        "adjoint": scatter_about(seeds[1], (N, N), 1.0, 6.0, ((0, 4), (1, 32)), jnp.float32),
    }


HIGHEST_PRECISION = lax.Precision.HIGHEST


def matmul(left_side, right_side):
    return jnp.dot(left_side, right_side, precision=HIGHEST_PRECISION, preferred_element_type=jnp.float32)


def tmatmul(left_side, right_side):
    return lax.dot_general(left_side, right_side, (((0,), (0,)), ((), ())), precision=HIGHEST_PRECISION, preferred_element_type=jnp.float32)


def lower_half(matrix):
    dimension = matrix.shape[0]
    positions = jnp.arange(dimension, dtype=jnp.int32)
    weight = jnp.where(positions[:, None] > positions[None, :], 1.0, jnp.where(positions[:, None] == positions[None, :], 0.5, 0.0))
    return matrix * weight.astype(matrix.dtype)


def inverse_lower(factor_block):
    dimension = factor_block.shape[0]
    if dimension == 1:
        return 1.0 / factor_block
    half_size = dimension // 2
    upper_inv = inverse_lower(factor_block[:half_size, :half_size])
    lower_inv = inverse_lower(factor_block[half_size:, half_size:])
    corner = -matmul(lower_inv, matmul(factor_block[half_size:, :half_size], upper_inv))
    zero_part = jnp.zeros((half_size, dimension - half_size), factor_block.dtype)
    top_rows = jnp.concatenate([upper_inv, zero_part], 1)
    bottom_rows = jnp.concatenate([corner, lower_inv], 1)
    return jnp.concatenate([top_rows, bottom_rows], 0)


def diagonal_adjoint(factor_block, block_bar, inverse):
    inner_part = lower_half(tmatmul(factor_block, block_bar))
    symmetric = tmatmul(inverse, matmul(inner_part, inverse))
    return lower_half(symmetric + symmetric.T)


def reference(factor, adjoint):
    row_ids = jnp.arange(N, dtype=jnp.int32)
    block_of = row_ids // NB
    offset = row_ids % NB
    global_row = ((block_of % BR) * ROWS_GRID + block_of // BR) * NB + offset
    global_col = ((block_of % BC) * COLS_GRID + block_of // BC) * NB + offset
    back_row = ((block_of % ROWS_GRID) * BR + block_of // ROWS_GRID) * NB + offset
    back_col = ((block_of % COLS_GRID) * BC + block_of // COLS_GRID) * NB + offset
    first_panel = factor[:, 0:NB][back_row]
    second_panel = factor[:, BC * NB:BC * NB + NB][back_row]
    first_bar = adjoint[:, 0:NB][back_row]
    second_bar = adjoint[:, BC * NB:BC * NB + NB][back_row]
    trailing = (row_ids >= 2 * NB)[:, None]
    panels = jnp.where(trailing, jnp.concatenate([first_panel, second_panel], 1), 0.0)
    by_row = panels[global_row]
    by_col = panels[global_col]

    def one_block(col_total, block_index):
        row_start = (block_index * NB).astype(jnp.int32)
        adjoint_strip = lax.dynamic_slice_in_dim(adjoint, row_start, NB, 0)
        strip_rows = lax.dynamic_slice_in_dim(global_row, row_start, NB, 0)
        keep = (strip_rows[:, None] >= global_col[None, :]) & (global_col[None, :] >= 2 * NB)
        masked = jnp.where(keep, adjoint_strip, 0.0)
        row_part = matmul(masked, by_col)
        col_total = col_total + tmatmul(masked, lax.dynamic_slice_in_dim(by_row, row_start, NB, 0))
        return col_total, row_part

    start_total = jnp.zeros((N, 2 * NB), jnp.float32)
    col_total, row_parts = lax.scan(one_block, start_total, jnp.arange(MB, dtype=jnp.int32))
    row_total = row_parts.reshape(N, 2 * NB)
    product = row_total[back_row] + col_total[back_col]

    l_second = jnp.tril(second_panel[NB:2 * NB])
    inv_second = inverse_lower(l_second)
    g_second = jnp.where(trailing, matmul(second_bar - product[:, NB:], inv_second), 0.0)
    k_second = jnp.tril(second_bar[NB:2 * NB]) - jnp.tril(tmatmul(g_second, panels[:, NB:]))
    e_second = diagonal_adjoint(l_second, k_second, inv_second)

    l_first = jnp.tril(first_panel[:NB])
    inv_first = inverse_lower(l_first)
    link_block = first_panel[NB:2 * NB]
    tail_rows = jnp.where(trailing, first_bar - product[:, :NB] - matmul(g_second, link_block), 0.0)
    head_rows = first_bar[NB:2 * NB] - matmul(e_second + e_second.T, link_block) - tmatmul(g_second, panels[:, :NB])
    residual = jnp.concatenate([jnp.zeros((NB, NB), jnp.float32), head_rows, tail_rows[2 * NB:]], 0)
    g_first = matmul(residual, inv_first)
    k_first = jnp.tril(first_bar[:NB]) - jnp.tril(tmatmul(g_first, first_panel))
    e_first = diagonal_adjoint(l_first, k_first, inv_first)

    left_half = jnp.concatenate([e_first, g_first[NB:]], 0)
    right_half = jnp.concatenate([jnp.zeros((NB, NB), jnp.float32), e_second, g_second[2 * NB:]], 0)
    whole = jnp.concatenate([left_half, right_half], 1)
    return whole[global_row]
```

```python
import jax
import jax.numpy as jnp
from jax import lax
from jax.experimental import pallas as pl
from jax.experimental.pallas import tpu as pltpu
from jax.sharding import PartitionSpec as P

NB = 256
HIGHEST = lax.Precision.HIGHEST
HIGH = lax.Precision.HIGH


def dot(a, b, precision=HIGHEST):
    return lax.dot_general(a, b, (((1,), (0,)), ((), ())), precision=precision, preferred_element_type=jnp.float32)


def tdot(a, b, precision=HIGHEST):
    return lax.dot_general(a, b, (((0,), (0,)), ((), ())), precision=precision, preferred_element_type=jnp.float32)


def grid_ids(n):
    return lax.broadcasted_iota(jnp.int32, (n, n), 0), lax.broadcasted_iota(jnp.int32, (n, n), 1)


def lower(x):
    i, j = grid_ids(x.shape[0])
    return jnp.where(i >= j, x, 0.0)


def lower_half(x):
    i, j = grid_ids(x.shape[0])
    return jnp.where(i > j, x, jnp.where(i == j, 0.5 * x, 0.0))


def inverse_lower(mats):
    n = mats[0].shape[0]
    i, j = grid_ids(n)
    found = []
    for m in mats:
        d = jnp.where(i == j, m, 0.0)
        found.append(jnp.where(i == j, 1.0 / jnp.where(i == j, m, 1.0), 0.0))
    k = 1
    while k < n:
        corner = (i // (2 * k) == j // (2 * k)) & (i // k > j // k)
        inner = [dot(jnp.where(corner, m, 0.0), x) for m, x in zip(mats, found)]
        found = [x - dot(x, y) for x, y in zip(found, inner)]
        k *= 2
    return found


MESH = pl.DeviceIdType.MESH
ROWS, HEAD, CHUNK = 4096, 512, 32
STEPS, LAG = 36, 5
DEPTH = ((0, 3, 4, 3, 3, 4, 5, 4, 2, 3, 4, 3, 1, 2, 3, 2), (0, 3, 2, 1, 3, 4, 3, 2, 4, 5, 4, 3, 3, 4, 3, 2),
         (0, 3, 4, 3, 1, 2, 3, 2, 2, 3, 4, 3, 3, 4, 5, 4), (0, 1, 2, 3, 3, 2, 3, 4, 4, 3, 4, 5, 3, 2, 3, 4))
TREE_OF_LINK = ((2, 3, 3, 1, 2, 2, 3, 1, 2, 2, 2, 2, 9, 0, 0, 0), (3, 3, 3, 9, 2, 2, 3, 1, 0, 0, 3, 1, 0, 3, 3, 1),
                (0, 3, 1, 1, 9, 2, 2, 2, 0, 0, 0, 0, 0, 3, 1, 0), (1, 9, 1, 1, 2, 3, 1, 1, 2, 3, 1, 2, 0, 3, 1, 0))
LINKS = ((1, 0), (0, 1), (3, 0), (0, 3))


def place():
    r, c = lax.axis_index("row"), lax.axis_index("col")
    return r, c, c // 8, (c // 2) % 4, c % 2


def at(r, y, z, k):
    return {"row": r, "col": (y * 4 + z) * 2 + k}


def pick(index, table):
    value = jnp.int32(table[0])
    for i, entry in enumerate(table[1:], 1):
        value = jnp.where(index == i, jnp.int32(entry), value)
    return value


def remote(src, dst, send, recv, device):
    return pltpu.make_async_remote_copy(
        src_ref=src, dst_ref=dst, send_sem=send, recv_sem=recv, device_id=device, device_id_type=MESH
    )


def meet(devices):
    barrier = pltpu.get_barrier_semaphore()
    for device in devices:
        pl.semaphore_signal(barrier, inc=1, device_id=device, device_id_type=MESH)
    pl.semaphore_wait(barrier, len(devices))


def broadcast_kernel(f_ref, p_ref, q_ref, send, sib_send, recv, sib_recv, x_send, x_recv, h_send, h_recv, own):
    r, c, y, z, k = place()
    chip = y * 4 + z
    sibling = at(r, y, z, 1 - k)
    nexts = [at(r, (y + dy) % 4, (z + dz) % 4, k) for dy, dz in LINKS]
    xs = [at((r + d) % 4, y, z, k) for d in (1, 3, 2)]
    meet(nexts + [sibling] + xs)
    depth = [pick(chip, row) for row in DEPTH]
    tree = [pick(chip, row) for row in TREE_OF_LINK]
    is_root = chip == 0

    def first_row(s, t):
        u = jnp.where(s < 8, s, s - 4)
        body = ((u % 8) * 2 + t // 2) * NB + (u // 8) * 64 + (t % 2) * CHUNK
        head = ROWS + ((s - 8) * 4 + t) * CHUNK
        return pl.multiple_of(jnp.where((s >= 8) & (s < 12), head, body), CHUNK)

    def pass_on(s, t, src, dst):
        remote(src, dst, sib_send.at[s, t], sib_recv.at[s, t], sibling).start()
        for d in range(4):
            @pl.when(tree[d] == t)
            def _():
                remote(src, dst, send.at[d, s], recv.at[s, t], nexts[d]).start()

    @pl.when(is_root)
    def _():
        pltpu.make_async_copy(f_ref.at[:, pl.ds(0, NB)], p_ref.at[k, pl.ds(0, ROWS), :], own.at[0]).start()
        for head in range(2):
            rows = p_ref.at[k, pl.ds(ROWS + head * NB, NB), :]
            block = f_ref.at[pl.ds(0, NB), pl.ds(0, NB)]

            @pl.when(r == head)
            def _():
                pltpu.make_async_copy(block, rows, own.at[1]).start()
                for i, device in enumerate(xs):
                    remote(block, rows, h_send.at[i], h_recv.at[head], device).start()

        def from_own(s, _):
            for t in range(4):
                rows = p_ref.at[k, pl.ds(first_row(s, t), CHUNK), :]
                pass_on(s, t, rows, rows)

        pltpu.make_async_copy(f_ref.at[:, pl.ds(0, NB)], p_ref.at[k, pl.ds(0, ROWS), :], own.at[0]).wait()
        lax.fori_loop(0, 8, from_own, None)
        for head in range(2):
            rows = p_ref.at[k, pl.ds(ROWS + head * NB, NB), :]

            @pl.when(r == head)
            def _():
                pltpu.make_async_copy(rows, rows, own.at[1]).wait()
                for i, device in enumerate(xs):
                    remote(rows, rows, h_send.at[i], h_recv.at[head], device).wait_send()

            @pl.when(r != head)
            def _():
                remote(rows, rows, h_send.at[0], h_recv.at[head], xs[0]).wait_recv()

        lax.fori_loop(8, STEPS, from_own, None)

    def forward(n, _):
        for t in range(4):
            s = n - LAG * (depth[t] - 1)

            @pl.when((s >= 0) & (s < STEPS))
            def _():
                rows = p_ref.at[k, pl.ds(first_row(s, t), CHUNK), :]
                remote(rows, rows, sib_send.at[s, t], recv.at[s, t], sibling).wait_recv()
                pass_on(s, t, rows, rows)

    m = c // 4
    stops = [8 + LAG * 4, 20 + LAG * 4, 28 + LAG * 4, 36 + LAG * 4]
    for j in range(4):
        @pl.when(jnp.logical_not(is_root))
        def _():
            lax.fori_loop(stops[j - 1] if j else 0, stops[j], forward, None)

        @pl.when(r == c % 4)
        def _():
            for b in range(2):
                row = pl.multiple_of((m + 8 * b) * NB + j * 64, 64)
                s = (j * 8 + 4 * b + m // 2) + (4 if j else 0)
                for half in range(2):
                    t = (m % 2) * 2 + half
                    got = p_ref.at[1 - k, pl.ds(row + half * CHUNK, CHUNK), :]
                    remote(got, got, sib_send.at[s, t], sib_recv.at[s, t], sibling).wait_recv()
                src = p_ref.at[:, pl.ds(row, 64), :]
                dst = q_ref.at[:, pl.ds(b * NB + j * 64, 64), :]
                pltpu.make_async_copy(src, dst, own.at[2 + j * 2 + b]).start()
                for i, device in enumerate(xs):
                    remote(src, dst, x_send.at[j, b, i], x_recv.at[j, b], device).start()

    def finish(s, _):
        for t in range(4):
            row = first_row(s, t)
            mine = p_ref.at[k, pl.ds(row, CHUNK), :]
            other = p_ref.at[1 - k, pl.ds(row, CHUNK), :]
            remote(mine, mine, sib_send.at[s, t], sib_recv.at[s, t], sibling).wait_send()
            u = jnp.where(s < 8, s, s - 4)
            block = (u % 8) * 2 + t // 2
            early = (r == c % 4) & ((s < 8) | (s >= 12)) & (block % 8 == m)

            @pl.when(jnp.logical_not(early))
            def _():
                remote(other, other, sib_send.at[s, t], sib_recv.at[s, t], sibling).wait_recv()
        for d in range(4):
            @pl.when(tree[d] < 4)
            def _():
                rows = p_ref.at[k, pl.ds(0, CHUNK), :]
                remote(rows, rows, send.at[d, s], recv.at[s, 0], nexts[d]).wait_send()

    lax.fori_loop(0, STEPS, finish, None)
    for j in range(4):
        for b in range(2):
            src = p_ref.at[:, pl.ds(0, 64), :]
            dst = q_ref.at[:, pl.ds(b * NB + j * 64, 64), :]

            @pl.when(r == c % 4)
            def _():
                pltpu.make_async_copy(src, dst, own.at[2 + j * 2 + b]).wait()
                for i, device in enumerate(xs):
                    remote(src, dst, x_send.at[j, b, i], x_recv.at[j, b], device).wait_send()

            @pl.when(r != c % 4)
            def _():
                remote(src, dst, x_send.at[j, b, 0], x_recv.at[j, b], xs[0]).wait_recv()


def broadcast(factor):
    dma = pltpu.SemaphoreType.DMA
    anywhere = pl.BlockSpec(memory_space=pl.ANY)
    return pl.pallas_call(
        broadcast_kernel,
        out_shape=(jax.ShapeDtypeStruct((2, ROWS + HEAD, NB), jnp.float32), jax.ShapeDtypeStruct((2, 512, NB), jnp.float32)),
        in_specs=[anywhere],
        out_specs=(pl.BlockSpec(memory_space=pltpu.VMEM),) * 2,
        scratch_shapes=[dma((4, STEPS)), dma((STEPS, 4)), dma((STEPS, 4)), dma((STEPS, 4)), dma((4, 2, 3)), dma((4, 2)),
                        dma((3,)), dma((2,)), dma((10,))],
        compiler_params=pltpu.CompilerParams(collective_id=1, has_side_effects=True, vmem_limit_bytes=40 << 20),
    )(factor)


def split(x):
    high = x.astype(jnp.bfloat16)
    return high, (x - high.astype(jnp.float32)).astype(jnp.bfloat16)


def dot3(a, b, dims):
    def one(x, w):
        return lax.dot_general(x, w, (dims, ((), ())), preferred_element_type=jnp.float32)
    return one(a[0], b[0]) + (one(a[0], b[1]) + one(a[1], b[0]))


def product_kernel(a_ref, p_ref, q_ref, w_ref, col_ref, m_ref, row_acc, qh, ql):
    step = pl.program_id(0)
    r, c = lax.axis_index("row"), lax.axis_index("col")
    block = 4 * step + r
    i, j = grid_ids(NB)

    @pl.when(step == 0)
    def _():
        col_ref[...] = jnp.zeros_like(col_ref)
        m_ref[...] = jnp.zeros_like(m_ref)
        for b in range(2):
            for k in range(2):
                qh[b, :, k * NB:(k + 1) * NB], ql[b, :, k * NB:(k + 1) * NB] = split(q_ref[k, b * NB:(b + 1) * NB, :])
        for head, (hr, hc, lo, side) in enumerate([(0, 0, 768, 0), (1, 0, 512, 0), (1, 1, 512, NB)]):
            @pl.when((r == hr) & (c == hc))
            def _():
                m_ref[lo:lo + NB, side:side + NB] = a_ref[:, :NB]

    row_acc[...] = jnp.zeros_like(row_acc)
    panel = split(jnp.concatenate([p_ref[0], p_ref[1]], 1))
    for b in range(2):
        column = 32 * b + c
        owner = (column < 2)

        @pl.when((block >= column) & (block >= 2))
        def _():
            tile = a_ref[:, b * NB:(b + 1) * NB]
            tile = jnp.where((block > column) | (i >= j), tile, 0.0)
            tile = split(tile)
            col_ref[b] += dot3(tile, panel, ((0,), (0,)))

            @pl.when(jnp.logical_not(owner))
            def _():
                row_acc[...] += dot3(tile, (qh[b], ql[b]), ((1,), (0,)))

    for side in range(2):
        part = slice(side * NB, (side + 1) * NB)
        own = jnp.where(c == side, a_ref[:, :NB], 0.0)
        w_ref[:, part] = own - row_acc[:, part]

    @pl.when(step == pl.num_programs(0) - 1)
    def _():
        for side in range(2):
            @pl.when(c == side)
            def _():
                m_ref[side * NB:(side + 1) * NB, :] = col_ref[0]

        @pl.when(c < 2)
        def _():
            col_ref[0] = jnp.zeros((NB, 512), jnp.float32)

        s = jnp.zeros((512, 512), jnp.float32)
        for b in range(2):
            s += dot3(split(col_ref[b]), (qh[b], ql[b]), ((0,), (0,)))
        m_ref[:512] += -s - s.T


def products(adjoint, p, q):
    return pl.pallas_call(
        product_kernel,
        out_shape=(jax.ShapeDtypeStruct((ROWS, 512), jnp.float32), jax.ShapeDtypeStruct((2, NB, 512), jnp.float32),
                   jax.ShapeDtypeStruct((1024, 512), jnp.float32)),
        grid=(16,),
        in_specs=[pl.BlockSpec((NB, 512), lambda a: (a, 0)), pl.BlockSpec((2, NB, NB), lambda a: (0, a, 0)),
                  pl.BlockSpec((2, 512, NB), lambda a: (0, 0, 0))],
        out_specs=(pl.BlockSpec((NB, 512), lambda a: (a, 0)), pl.BlockSpec((2, NB, 512), lambda a: (0, 0, 0)),
                   pl.BlockSpec((1024, 512), lambda a: (0, 0))),
        scratch_shapes=[pltpu.VMEM((NB, 512), jnp.float32), pltpu.VMEM((2, NB, 512), jnp.bfloat16), pltpu.VMEM((2, NB, 512), jnp.bfloat16)],
        compiler_params=pltpu.CompilerParams(vmem_limit_bytes=40 << 20),
    )(adjoint, p, q)


def reduce_kernel(w_ref, col_ref, m_ref, h_ref, o_ref, top_ref, acc, sib, r1, r2, part, t1, t2, v, col_x, col_p, m_a, m_s, m_x, m_b,
                  m_y, m_c, m_z, m_f, s0, s1, s2, s3, s4, sc, sp, sm, g1, g2, gs):
    r, c, y, z, k = place()
    sibling = at(r, y, z, 1 - k)
    xp = [at((r + d) % 4, y, z, k) for d in (1, 2, 3)]
    yp = [at(r, (y + d) % 4, z, k) for d in (1, 2, 3)]
    zp = [at(r, y, (z + d) % 4, k) for d in (1, 2, 3)]
    own_col = c % 4
    m_id = c // 4
    chip = y * 4 + z
    source = (4 * chip + r) % 32
    barrier = pltpu.get_barrier_semaphore()
    for device in xp + yp + zp + [sibling]:
        pl.semaphore_signal(barrier, inc=1, device_id=device, device_id_type=MESH)
    others = jnp.int32(0)
    targets = [2 * (m_id + 8 * b) + h for b in range(2) for h in range(2)]
    for target in targets:
        others += jnp.where((r == own_col) & (target != c), 1, 0).astype(jnp.int32)

    @pl.when(source != c)
    def _():
        pl.semaphore_signal(barrier, inc=1, device_id={"row": r, "col": source}, device_id_type=MESH)
    pl.semaphore_wait(barrier, 10 + others)

    sent = []

    def send(src, dst, sems, index, device):
        copy = remote(src, dst, sems.at[(0, *index)], sems.at[(1, *index)], device)
        copy.start()
        sent.append(copy)

    def arrive(dst, sems, index):
        remote(dst, dst, sems.at[(0, *index)], sems.at[(1, *index)], sibling).wait_recv()

    first = [z, y]
    second = [y, z]
    first_peers, second_peers = [zp, yp], [yp, zp]

    def w_shard(f, h, i):
        return w_ref.at[:, i, h, 0] if f == 0 else w_ref.at[i, :, h, 1]

    send(m_ref.at[1 - k], m_s, sm, (0, 0), sibling)
    for j in (2, 1, 3, 0):
        for f in range(2):
            i = (first[f] + j) % 4
            send(w_shard(f, 1 - k, i), sib.at[f, i], s0, (f, j), sibling)

    @pl.when(r != own_col)
    def _():
        slot = (own_col - r + 4) % 4 - 1
        remote(col_ref, col_x.at[slot], sc.at[0, 0], sc.at[1, slot], {"row": own_col, "col": c}).start()

    arrive(m_s, sm, (0, 0))
    m_a[...] = m_ref[k] + m_s[...]
    for d in range(3):
        send(m_a.at[(r + d + 1) % 4], m_x.at[d], sm, (1, d), xp[d])

    for j in (2, 1, 3, 0):
        for f in range(2):
            i = (first[f] + j) % 4
            arrive(sib.at[f, i], s0, (f, j))
            acc[f, i] = w_shard(f, k, i)[...] + sib[f, i]
            up, down = first_peers[f][0], first_peers[f][2]
            if j == 2:
                send(acc.at[f, i, pl.ds(0, 2)], r1.at[f, 0], s1, (f, 0), up)
                send(acc.at[f, i, pl.ds(2, 2)], r1.at[f, 1], s1, (f, 1), down)
            if j == 1:
                send(acc.at[f, i, pl.ds(2, 2)], r2.at[f, 0, pl.ds(2, 2)], s2, (f, 0, 1), up)
            if j == 3:
                send(acc.at[f, i, pl.ds(0, 2)], r2.at[f, 1, pl.ds(0, 2)], s2, (f, 1, 0), down)
    for f in range(2):
        up, down = first_peers[f][0], first_peers[f][2]
        i = (first[f] + 1) % 4
        arrive(r1.at[f, 0], s1, (f, 0))
        acc[f, i, 0:2] = acc[f, i, 0:2] + r1[f, 0]
        send(acc.at[f, i, pl.ds(0, 2)], r2.at[f, 0, pl.ds(0, 2)], s2, (f, 0, 0), up)
        i = (first[f] + 3) % 4
        arrive(r1.at[f, 1], s1, (f, 1))
        acc[f, i, 2:4] = acc[f, i, 2:4] + r1[f, 1]
        send(acc.at[f, i, pl.ds(2, 2)], r2.at[f, 1, pl.ds(2, 2)], s2, (f, 1, 1), down)

    v[0], v[1] = inverse_lower([lower(h_ref[0, :NB]), lower(h_ref[1, NB:])])

    for d in range(3):
        arrive(m_x.at[d], sm, (1, d))
    m_b[...] = (m_a[r] + m_x[0] + (m_x[1] + m_x[2])).reshape(4, 32, 512)
    for d in range(3):
        send(m_b.at[(y + d + 1) % 4], m_y.at[d], sm, (2, d), yp[d])

    @pl.when(r == own_col)
    def _():
        for d in range(3):
            remote(col_x.at[d], col_x.at[d], sc.at[0, 0], sc.at[1, d], sibling).wait_recv()
        col_x[0] = col_ref[...] + col_x[0] + (col_x[1] + col_x[2])
        for index, target in enumerate(targets):
            b, h = index // 2, index % 2

            @pl.when(target != c)
            def _():
                remote(col_x.at[0, b, h], col_p, sp.at[0, index], sp.at[1, 0], {"row": r, "col": target}).start()

            @pl.when(target == c)
            def _():
                col_p[...] = col_x[0, b, h]

    for f in range(2):
        for side in range(2):
            for half in range(2):
                arrive(r2.at[f, side, pl.ds(2 * half, 2)], s2, (f, side, half))
        part[f] = acc[f, first[f]] + (r2[f, 0] + r2[f, 1])
        up, down = second_peers[f][0], second_peers[f][2]
        i = (second[f] + 2) % 4
        send(part.at[f, i, pl.ds(0, 32)], t1.at[f, 0], s3, (f, 0), up)
        send(part.at[f, i, pl.ds(32, 32)], t1.at[f, 1], s3, (f, 1), down)
        i = (second[f] + 1) % 4
        send(part.at[f, i, pl.ds(32, 32)], t2.at[f, 0, pl.ds(32, 32)], s4, (f, 0, 1), up)
        i = (second[f] + 3) % 4
        send(part.at[f, i, pl.ds(0, 32)], t2.at[f, 1, pl.ds(0, 32)], s4, (f, 1, 0), down)
    for d in range(3):
        arrive(m_y.at[d], sm, (2, d))
    m_c[...] = (m_b[y] + m_y[0] + (m_y[1] + m_y[2])).reshape(4, 8, 512)
    for d in range(3):
        send(m_c.at[(z + d + 1) % 4], m_z.at[d], sm, (3, d), zp[d])
    for f in range(2):
        up, down = second_peers[f][0], second_peers[f][2]
        i = (second[f] + 1) % 4
        arrive(t1.at[f, 0], s3, (f, 0))
        part[f, i, 0:32] = part[f, i, 0:32] + t1[f, 0]
        send(part.at[f, i, pl.ds(0, 32)], t2.at[f, 0, pl.ds(0, 32)], s4, (f, 0, 0), up)
        i = (second[f] + 3) % 4
        arrive(t1.at[f, 1], s3, (f, 1))
        part[f, i, 32:64] = part[f, i, 32:64] + t1[f, 1]
        send(part.at[f, i, pl.ds(32, 32)], t2.at[f, 1, pl.ds(32, 32)], s4, (f, 1, 1), down)
    for d in range(3):
        arrive(m_z.at[d], sm, (3, d))
    m_f[k, r, y, z] = m_c[z] + m_z[0] + (m_z[1] + m_z[2])
    for d in range(3):
        send(m_f.at[k, r, y, z], m_f.at[k, r, y, z], sm, (4, d), zp[d])

    @pl.when(source != c)
    def _():
        remote(col_p, col_p, sp.at[0, 0], sp.at[1, 0], sibling).wait_recv()

    def piece(f, i1, i2, half=None, h=None):
        h = k if h is None else h
        ref = o_ref.at[i2, i1, h, f] if f == 0 else o_ref.at[i1, i2, h, f]
        return ref if half is None else ref.at[pl.ds(half * 32, 32)]

    link = h_ref[0, NB:]
    for f in range(2):
        for side in range(2):
            for half in range(2):
                arrive(t2.at[f, side, pl.ds(32 * half, 32)], s4, (f, side, half))
        rows = part[f, second[f]] + (t2[f, 0] + t2[f, 1]) - col_p[f * 64:f * 64 + 64, :]
        last = dot(rows[:, NB:], v[1])
        piece(f, first[f], second[f])[...] = jnp.concatenate([dot(rows[:, :NB] - dot(last, link), v[0]), last], 1)
        mine = piece(f, first[f], second[f])
        send(mine, mine, g1, (f, 0), second_peers[f][0])
        send(mine, mine, g1, (f, 1), second_peers[f][2])
        for s, to in ((0, 0), (1, 2)):
            send(mine, mine, g2, (f, 0, s), first_peers[f][to])
        send(mine, mine, gs, (f, 0, 0), sibling)

    zs = [(z + 4 - d) % 4 for d in (1, 2, 3)]
    for d in range(3):
        arrive(m_f.at[k, r, y, zs[d]], sm, (4, d))
    for d in range(3):
        send(m_f.at[k, r, y], m_f.at[k, r, y], sm, (5, d), yp[d])

    for f in range(2):
        i1, i2 = first[f], second[f]
        back, ahead = piece(f, i1, (i2 + 3) % 4), piece(f, i1, (i2 + 1) % 4)
        arrive(back, g1, (f, 0))
        half = piece(f, i1, (i2 + 3) % 4, 0)
        send(half, half, g1, (f, 2), second_peers[f][0])
        arrive(ahead, g1, (f, 1))
        half = piece(f, i1, (i2 + 1) % 4, 1)
        send(half, half, g1, (f, 3), second_peers[f][2])
        for e, ref in ((3, back), (1, ahead)):
            for s, to in ((0, 0), (1, 2)):
                send(ref, ref, g2, (f, e, s), first_peers[f][to])
            send(ref, ref, gs, (f, e, 0), sibling)

    ys = [(y + 4 - d) % 4 for d in (1, 2, 3)]
    for d in range(3):
        arrive(m_f.at[k, r, ys[d]], sm, (5, d))
    for d in range(3):
        send(m_f.at[k, r], m_f.at[k, r], sm, (6, d), xp[d])

    def relay(f, e):
        i1, i2 = first[f], (second[f] + e) % 4
        for s, near, to in ((0, 3, 0), (1, 1, 2)):
            got = piece(f, (i1 + near) % 4, i2)
            arrive(got, g2, (f, e, s))
            half = piece(f, (i1 + near) % 4, i2, s)
            send(half, half, g2, (f, e, 2 + s), first_peers[f][to])
            send(got, got, gs, (f, e, 1 + s), sibling)

    for f in range(2):
        relay(f, 0)
    for f in range(2):
        i1, i2 = first[f], (second[f] + 2) % 4
        for s in range(2):
            arrive(piece(f, i1, i2, s), g1, (f, 2 + s))
        far = piece(f, i1, i2)
        for s, to in ((0, 0), (1, 2)):
            send(far, far, g2, (f, 2, s), first_peers[f][to])
        send(far, far, gs, (f, 2, 0), sibling)
    for e in (3, 1):
        for f in range(2):
            relay(f, e)
    rs = [(r + 4 - d) % 4 for d in (1, 2, 3)]
    for d in range(3):
        arrive(m_f.at[k, rs[d]], sm, (6, d))
    send(m_f.at[k], m_f.at[k], sm, (7, 0), sibling)
    for f in range(2):
        relay(f, 2)
    for e in (0, 3, 1, 2):
        for f in range(2):
            i1, i2 = first[f], (second[f] + e) % 4
            for s in range(2):
                arrive(piece(f, (i1 + 2) % 4, i2, s), g2, (f, e, 2 + s))
            far = piece(f, (i1 + 2) % 4, i2)
            send(far, far, gs, (f, e, 3), sibling)

    arrive(m_f.at[1 - k], sm, (7, 0))

    @pl.when(r < 2)
    def _():
        m = m_f[...].reshape(1024, 512)
        l0, l1, v0, v1 = lower(h_ref[0, :NB]), lower(h_ref[1, NB:]), v[0], v[1]
        g1q = tdot(v1, m[NB:512])
        g1q0, g1q1 = g1q[:, :NB], g1q[:, NB:]
        k1 = lower(m[512:768, NB:]) - lower(g1q1)
        e1 = tdot(v1, dot(lower_half(tdot(l1, k1)), v1))
        e1 = lower_half(e1 + e1.T)
        g01 = dot(m[512:768, :NB] - dot(e1 + e1.T, link) - g1q0, v0)

        @pl.when(r == 1)
        def _():
            top_ref[:, :NB] = g01
            top_ref[:, NB:] = e1

        @pl.when(r == 0)
        def _():
            g0q0 = tdot(v0, m[:NB, :NB] - tdot(link, g1q0)) + tdot(g01, link)
            k0 = lower(m[768:, :NB]) - lower(g0q0)
            e0 = tdot(v0, dot(lower_half(tdot(l0, k0)), v0))
            top_ref[:, :NB] = lower_half(e0 + e0.T)
            top_ref[:, NB:] = jnp.zeros((NB, NB), jnp.float32)

    @pl.when(r >= 2)
    def _():
        top_ref[...] = jnp.zeros((NB, 512), jnp.float32)

    for e in range(4):
        for f in range(2):
            i1, i2 = first[f], (second[f] + e) % 4
            for s, near in enumerate((0, 3, 1, 2)):
                arrive(piece(f, (i1 + near) % 4, i2, None, 1 - k), gs, (f, e, s))
    for copy in sent:
        copy.wait_send()

    @pl.when(r != own_col)
    def _():
        remote(col_ref, col_ref, sc.at[0, 0], sc.at[1, 0], sibling).wait_send()

    @pl.when(r == own_col)
    def _():
        for index, target in enumerate(targets):
            @pl.when(target != c)
            def _():
                remote(col_p, col_p, sp.at[0, index], sp.at[1, 0], sibling).wait_send()


def reduce_and_gather(w, col_part, m_part, heads):
    f32 = jnp.float32
    vmem, dma = pltpu.VMEM, pltpu.SemaphoreType.DMA
    here = pl.BlockSpec(memory_space=pltpu.VMEM)
    o, top = pl.pallas_call(
        reduce_kernel,
        out_shape=(jax.ShapeDtypeStruct((4, 4, 2, 2, 64, 512), f32), jax.ShapeDtypeStruct((NB, 512), f32)),
        in_specs=[here] * 4,
        out_specs=(here, here),
        scratch_shapes=[
            vmem((2, 4, 4, 64, 512), f32), vmem((2, 4, 4, 64, 512), f32), vmem((2, 2, 2, 64, 512), f32), vmem((2, 2, 4, 64, 512), f32),
            vmem((2, 4, 64, 512), f32), vmem((2, 2, 32, 512), f32), vmem((2, 2, 64, 512), f32), vmem((2, NB, NB), f32),
            vmem((3, 2, 2, 128, 512), f32), vmem((128, 512), f32), vmem((4, 128, 512), f32), vmem((4, 128, 512), f32),
            vmem((3, 128, 512), f32), vmem((4, 32, 512), f32), vmem((3, 32, 512), f32), vmem((4, 8, 512), f32), vmem((3, 8, 512), f32),
            vmem((2, 4, 4, 4, 8, 512), f32),
            dma((2, 2, 4)), dma((2, 2, 2)), dma((2, 2, 2, 2)), dma((2, 2, 2)), dma((2, 2, 2, 2)), dma((2, 3)), dma((2, 4)),
            dma((2, 8, 3)), dma((2, 2, 4)), dma((2, 2, 4, 4)), dma((2, 2, 4, 4)),
        ],
        compiler_params=pltpu.CompilerParams(collective_id=2, has_side_effects=True, vmem_limit_bytes=60 << 20),
    )(w.reshape(4, 4, 2, 2, 64, 512), col_part.reshape(2, 2, 128, 512), m_part.reshape(2, 4, 128, 512), heads)
    return o.reshape(ROWS, 512), top


def local(factor, adjoint):
    row_id = lax.axis_index("row")
    p, q = broadcast(factor)
    w, col_part, m_part = products(adjoint, p, q)
    out, top = reduce_and_gather(w, col_part, m_part, p[:, ROWS:])
    return jnp.concatenate([jnp.where(row_id < 2, top, out[:NB]), out[NB:]], 0)


def solution(mesh):
    placed = (P("row", "col"), P("row", "col"))
    return jax.shard_map(local, mesh=mesh, in_specs=placed, out_specs=P("row", None), check_vma=False)
```

```python
import jax
import jax.numpy as jnp
from jax import lax
from jax.experimental import pallas as pl
from jax.experimental.pallas import tpu as pltpu
from jax.sharding import PartitionSpec as P

NB = 256
HIGHEST = lax.Precision.HIGHEST
HIGH = lax.Precision.HIGH


def dot(a, b, precision=HIGHEST):
    return lax.dot_general(a, b, (((1,), (0,)), ((), ())), precision=precision, preferred_element_type=jnp.float32)


def tdot(a, b, precision=HIGHEST):
    return lax.dot_general(a, b, (((0,), (0,)), ((), ())), precision=precision, preferred_element_type=jnp.float32)


def grid_ids(n):
    return lax.broadcasted_iota(jnp.int32, (n, n), 0), lax.broadcasted_iota(jnp.int32, (n, n), 1)


def lower(x):
    i, j = grid_ids(x.shape[0])
    return jnp.where(i >= j, x, 0.0)


def lower_half(x):
    i, j = grid_ids(x.shape[0])
    return jnp.where(i > j, x, jnp.where(i == j, 0.5 * x, 0.0))


MESH = pl.DeviceIdType.MESH
ROWS, HEAD, CHUNK = 4096, 512, 32
STEPS, LAG, AHEAD = 36, 5, 16
DEPTH = ((0, 3, 4, 3, 3, 4, 5, 4, 2, 3, 4, 3, 1, 2, 3, 2), (0, 3, 2, 1, 3, 4, 3, 2, 4, 5, 4, 3, 3, 4, 3, 2),
         (0, 3, 4, 3, 1, 2, 3, 2, 2, 3, 4, 3, 3, 4, 5, 4), (0, 1, 2, 3, 3, 2, 3, 4, 4, 3, 4, 5, 3, 2, 3, 4))
TREE_OF_LINK = ((2, 3, 3, 1, 2, 2, 3, 1, 2, 2, 2, 2, 9, 0, 0, 0), (3, 3, 3, 9, 2, 2, 3, 1, 0, 0, 3, 1, 0, 3, 3, 1),
                (0, 3, 1, 1, 9, 2, 2, 2, 0, 0, 0, 0, 0, 3, 1, 0), (1, 9, 1, 1, 2, 3, 1, 1, 2, 3, 1, 2, 0, 3, 1, 0))
LINKS = ((1, 0), (0, 1), (3, 0), (0, 3))


def place():
    r, c = lax.axis_index("row"), lax.axis_index("col")
    return r, c, c // 8, (c // 2) % 4, c % 2


def at(r, y, z, k):
    return {"row": r, "col": (y * 4 + z) * 2 + k}


def pick(index, table):
    value = jnp.int32(table[0])
    for i, entry in enumerate(table[1:], 1):
        value = jnp.where(index == i, jnp.int32(entry), value)
    return value


def remote(src, dst, send, recv, device):
    return pltpu.make_async_remote_copy(
        src_ref=src, dst_ref=dst, send_sem=send, recv_sem=recv, device_id=device, device_id_type=MESH
    )


def meet(devices):
    barrier = pltpu.get_barrier_semaphore()
    for device in devices:
        pl.semaphore_signal(barrier, inc=1, device_id=device, device_id_type=MESH)
    pl.semaphore_wait(barrier, len(devices))


def broadcast_kernel(f_ref, p_ref, q_ref, send, sib_send, recv, sib_recv, x_send, x_recv, h_send, h_recv, own):
    r, c, y, z, k = place()
    chip = y * 4 + z
    sibling = at(r, y, z, 1 - k)
    nexts = [at(r, (y + dy) % 4, (z + dz) % 4, k) for dy, dz in LINKS]
    xs = [at((r + d) % 4, y, z, k) for d in (1, 3, 2)]
    load = pltpu.make_async_copy(f_ref.at[:, pl.ds(0, NB)], p_ref.at[k, pl.ds(0, ROWS), :], own.at[0])

    @pl.when(chip == 0)
    def _():
        load.start()

    meet(nexts + [sibling] + xs)
    depth = [pick(chip, row) for row in DEPTH]
    tree = [pick(chip, row) for row in TREE_OF_LINK]
    is_root = chip == 0

    def first_row(s, t):
        u = jnp.where(s < AHEAD, s, s - 4)
        body = ((u % 8) * 2 + t // 2) * NB + (u // 8) * 64 + (t % 2) * CHUNK
        head = ROWS + ((s - AHEAD) * 4 + t) * CHUNK
        return pl.multiple_of(jnp.where((s >= AHEAD) & (s < AHEAD + 4), head, body), CHUNK)

    def pass_on(s, t, src, dst):
        for d in range(4):
            @pl.when(tree[d] == t)
            def _():
                remote(src, dst, send.at[d, s], recv.at[s, t], nexts[d]).start()
        remote(src, dst, sib_send.at[s, t], sib_recv.at[s, t], sibling).start()

    @pl.when(is_root)
    def _():
        for head in range(2):
            rows = p_ref.at[k, pl.ds(ROWS + head * NB, NB), :]
            block = f_ref.at[pl.ds(0, NB), pl.ds(0, NB)]

            @pl.when(r == head)
            def _():
                pltpu.make_async_copy(block, rows, own.at[1]).start()
                for i, device in enumerate(xs):
                    remote(block, rows, h_send.at[i], h_recv.at[head], device).start()

        def from_own(s, _):
            for t in range(4):
                rows = p_ref.at[k, pl.ds(first_row(s, t), CHUNK), :]
                pass_on(s, t, rows, rows)

        load.wait()
        lax.fori_loop(0, AHEAD, from_own, None)
        for head in range(2):
            rows = p_ref.at[k, pl.ds(ROWS + head * NB, NB), :]

            @pl.when(r == head)
            def _():
                pltpu.make_async_copy(rows, rows, own.at[1]).wait()
                for i, device in enumerate(xs):
                    remote(rows, rows, h_send.at[i], h_recv.at[head], device).wait_send()

            @pl.when(r != head)
            def _():
                remote(rows, rows, h_send.at[0], h_recv.at[head], xs[0]).wait_recv()

        lax.fori_loop(AHEAD, STEPS, from_own, None)

    def forward(n, _):
        for t in range(4):
            s = n - LAG * (depth[t] - 1)

            @pl.when((s >= 0) & (s < STEPS))
            def _():
                rows = p_ref.at[k, pl.ds(first_row(s, t), CHUNK), :]
                remote(rows, rows, sib_send.at[s, t], recv.at[s, t], sibling).wait_recv()
                pass_on(s, t, rows, rows)

    m = c // 4
    stops = [8 * j + 8 + (4 if 8 * j + 8 > AHEAD else 0) + LAG * 4 for j in range(4)]
    for j in range(4):
        @pl.when(jnp.logical_not(is_root))
        def _():
            lax.fori_loop(stops[j - 1] if j else 0, stops[j], forward, None)

        @pl.when(r == c % 4)
        def _():
            for b in range(2):
                row = pl.multiple_of((m + 8 * b) * NB + j * 64, 64)
                s = (j * 8 + 4 * b + m // 2) + (4 if 8 * j >= AHEAD else 0)
                for half in range(2):
                    t = (m % 2) * 2 + half
                    got = p_ref.at[1 - k, pl.ds(row + half * CHUNK, CHUNK), :]
                    remote(got, got, sib_send.at[s, t], sib_recv.at[s, t], sibling).wait_recv()
                src = p_ref.at[:, pl.ds(row, 64), :]
                dst = q_ref.at[:, pl.ds(b * NB + j * 64, 64), :]
                pltpu.make_async_copy(src, dst, own.at[2 + j * 2 + b]).start()
                for i, device in enumerate(xs):
                    remote(src, dst, x_send.at[j, b, i], x_recv.at[j, b], device).start()

    def finish(s, _):
        for t in range(4):
            row = first_row(s, t)
            mine = p_ref.at[k, pl.ds(row, CHUNK), :]
            other = p_ref.at[1 - k, pl.ds(row, CHUNK), :]
            remote(mine, mine, sib_send.at[s, t], sib_recv.at[s, t], sibling).wait_send()
            u = jnp.where(s < AHEAD, s, s - 4)
            block = (u % 8) * 2 + t // 2
            early = (r == c % 4) & ((s < AHEAD) | (s >= AHEAD + 4)) & (block % 8 == m)

            @pl.when(jnp.logical_not(early))
            def _():
                remote(other, other, sib_send.at[s, t], sib_recv.at[s, t], sibling).wait_recv()
        for d in range(4):
            @pl.when(tree[d] < 4)
            def _():
                rows = p_ref.at[k, pl.ds(0, CHUNK), :]
                remote(rows, rows, send.at[d, s], recv.at[s, 0], nexts[d]).wait_send()

    lax.fori_loop(0, STEPS, finish, None)
    for j in range(4):
        for b in range(2):
            src = p_ref.at[:, pl.ds(0, 64), :]
            dst = q_ref.at[:, pl.ds(b * NB + j * 64, 64), :]

            @pl.when(r == c % 4)
            def _():
                pltpu.make_async_copy(src, dst, own.at[2 + j * 2 + b]).wait()
                for i, device in enumerate(xs):
                    remote(src, dst, x_send.at[j, b, i], x_recv.at[j, b], device).wait_send()

            @pl.when(r != c % 4)
            def _():
                remote(src, dst, x_send.at[j, b, 0], x_recv.at[j, b], xs[0]).wait_recv()


def broadcast(factor):
    dma = pltpu.SemaphoreType.DMA
    return pl.pallas_call(
        broadcast_kernel,
        out_shape=(jax.ShapeDtypeStruct((2, ROWS + HEAD, NB), jnp.float32), jax.ShapeDtypeStruct((2, 512, NB), jnp.float32)),
        in_specs=[pl.BlockSpec(memory_space=pltpu.HBM)],
        out_specs=(pl.BlockSpec(memory_space=pltpu.VMEM),) * 2,
        scratch_shapes=[dma((4, STEPS)), dma((STEPS, 4)), dma((STEPS, 4)), dma((STEPS, 4)), dma((4, 2, 3)), dma((4, 2)),
                        dma((3,)), dma((2,)), dma((10,))],
        compiler_params=pltpu.CompilerParams(collective_id=1, has_side_effects=True, vmem_limit_bytes=60 << 20),
    )(factor)


def split(x):
    high = x.astype(jnp.bfloat16)
    return high, (x - high.astype(jnp.float32)).astype(jnp.bfloat16)


def dot3(a, b, dims):
    def one(x, w):
        return lax.dot_general(x, w, (dims, ((), ())), preferred_element_type=jnp.float32)
    return one(a[0], b[0]) + (one(a[0], b[1]) + one(a[1], b[0]))


def inverse_first(mats):
    i, j = grid_ids(NB)
    d = [jnp.where(i == j, 1.0 / jnp.where(i == j, m, 1.0), 0.0) for m in mats]
    return inverse_level(mats, d, 1)


def inverse_level(mats, found, size):
    i, j = grid_ids(NB)
    corner = (i // (2 * size) == j // (2 * size)) & (i // size > j // size)
    inner = [dot(jnp.where(corner, m, 0.0), x) for m, x in zip(mats, found)]
    return [x - dot(x, y) for x, y in zip(found, inner)]


def main_kernel(a_hbm, p_hbm, q_ref, o_ref, top_ref, a_ref, p_ref, h_ref, qh, ql, row_acc, w_ref, col_ref, m_ref, acc, sib, r1, r2, part, t1, t2, v, col_x, col_p, m_a, m_s, m_x, m_b,
                  m_y, m_c, m_z, m_f, sl, s0, s1, s2, s3, s4, sc, sp, sm, g1, g2, gs):
    r, c, y, z, k = place()
    sibling = at(r, y, z, 1 - k)
    xp = [at((r + d) % 4, y, z, k) for d in (1, 2, 3)]
    yp = [at(r, (y + d) % 4, z, k) for d in (1, 2, 3)]
    zp = [at(r, y, (z + d) % 4, k) for d in (1, 2, 3)]
    own_col = c % 4
    m_id = c // 4
    chip = y * 4 + z
    source = (4 * chip + r) % 32
    barrier = pltpu.get_barrier_semaphore()
    for device in xp + yp + zp + [sibling]:
        pl.semaphore_signal(barrier, inc=1, device_id=device, device_id_type=MESH)
    others = jnp.int32(0)
    targets = [2 * (m_id + 8 * b) + h for b in range(2) for h in range(2)]
    for target in targets:
        others += jnp.where((r == own_col) & (target != c), 1, 0).astype(jnp.int32)

    @pl.when(source != c)
    def _():
        pl.semaphore_signal(barrier, inc=1, device_id={"row": r, "col": source}, device_id_type=MESH)

    def load_a(a):
        rows = pl.ds(pl.multiple_of(a * NB, NB), NB)
        return pltpu.make_async_copy(a_hbm.at[rows], a_ref.at[a], sl.at[a])

    def load_p(a):
        rows = pl.ds(pl.multiple_of(a * NB, NB), NB)
        return pltpu.make_async_copy(p_hbm.at[:, rows], p_ref.at[a % 2], sl.at[16 + a % 2])

    load_h = pltpu.make_async_copy(p_hbm.at[:, pl.ds(ROWS, HEAD)], h_ref, sl.at[18])
    load_p(0).start()
    for a in range(16):
        load_a(a).start()
    load_h.start()
    i_ids, j_ids = grid_ids(NB)
    col_ref[...] = jnp.zeros_like(col_ref)
    m_ref[...] = jnp.zeros_like(m_ref)
    for b in range(2):
        for side in range(2):
            qh[b, :, side * NB:(side + 1) * NB], ql[b, :, side * NB:(side + 1) * NB] = split(q_ref[side, b * NB:(b + 1) * NB, :])

    def tile_of(a, b):
        column = 32 * b + c
        tile = a_ref[a, :, b * NB:(b + 1) * NB]
        return split(jnp.where((4 * a + r > column) | (i_ids >= j_ids), tile, 0.0))

    def column_step(a, _):
        @pl.when(a < 15)
        def _():
            load_p(a + 1).start()
        load_a(a).wait()
        load_p(a).wait()
        panel = split(jnp.concatenate([p_ref[a % 2, 0], p_ref[a % 2, 1]], 1))
        for b in range(2):
            @pl.when((4 * a + r >= 32 * b + c) & (4 * a + r >= 2))
            def _():
                col_ref[b] += dot3(tile_of(a, b), panel, ((0,), (0,))).reshape(2, 128, 512)

    lax.fori_loop(0, 16, column_step, None)
    for hr, hc, lo, side in ((0, 0, 2, 0), (1, 0, 0, 0), (1, 1, 0, NB)):
        @pl.when((r == hr) & (c == hc))
        def _():
            m_ref[1, lo:lo + 2, :, side:side + NB] = a_ref[0, :, :NB].reshape(2, 128, NB)
    for side in range(2):
        @pl.when(c == side)
        def _():
            m_ref[0, 2 * side:2 * side + 2] = col_ref[0]

    @pl.when(c < 2)
    def _():
        col_ref[0] = jnp.zeros((2, 128, 512), jnp.float32)

    gram = jnp.zeros((512, 512), jnp.float32)
    for b in range(2):
        gram += dot3(split(col_ref[b].reshape(NB, 512)), (qh[b], ql[b]), ((0,), (0,)))
    m_ref[0] += (-gram - gram.T).reshape(4, 128, 512)
    load_h.wait()
    pl.semaphore_wait(barrier, 10 + others)

    sent = []

    def send(src, dst, sems, index, device):
        copy = remote(src, dst, sems.at[(0, *index)], sems.at[(1, *index)], device)
        copy.start()
        sent.append(copy)

    def arrive(dst, sems, index):
        remote(dst, dst, sems.at[(0, *index)], sems.at[(1, *index)], sibling).wait_recv()

    def invert(stage):
        low = [lower(h_ref[0, :NB]), lower(h_ref[1, NB:])]
        found = inverse_first(low) if stage == 0 else [v[0], v[1]]
        for size in ((2, 4), (8, 16, 32), (64, 128))[stage]:
            found = inverse_level(low, found, size)
        v[0], v[1] = found

    first = [z, y]
    second = [y, z]
    first_peers, second_peers = [zp, yp], [yp, zp]

    def w_shard(f, h, i):
        return w_ref.at[:, i, h, 0] if f == 0 else w_ref.at[i, :, h, 1]

    send(m_ref.at[1 - k], m_s, sm, (0, 0), sibling)
    arrive(m_s, sm, (0, 0))
    m_a[...] = m_ref[k] + m_s[...]
    for d in range(3):
        send(m_a.at[(r + d + 1) % 4], m_x.at[d], sm, (1, d), xp[d])

    gap = (own_col - r + 4) % 4

    def col_copy(b, slot, device, which):
        return remote(col_ref.at[b], col_x.at[slot, b], sc.at[0, which], sc.at[1, 2 * slot + b], device)

    @pl.when(gap == 2)
    def _():
        col_copy(0, 2, xp[2], 0).start()
        col_copy(1, 2, xp[0], 1).start()

    @pl.when(gap == 3)
    def _():
        col_copy(1, 0, xp[2], 0).start()

    @pl.when(gap == 1)
    def _():
        col_copy(0, 1, xp[0], 0).start()

    def row_step(row_y, row_z):
        a = 4 * row_y + row_z
        row_acc[...] = jnp.zeros_like(row_acc)
        for b in range(2):
            column = 32 * b + c

            @pl.when((4 * a + r >= column) & (column >= 2))
            def _():
                row_acc[...] += dot3(tile_of(a, b), (qh[b], ql[b]), ((1,), (0,)))
        for side in range(2):
            part_of = slice(side * NB, (side + 1) * NB)
            own = jnp.where(c == side, a_ref[a, :, :NB], 0.0)
            w_ref[row_y, row_z, :, :, :, part_of] = (own - row_acc[:, part_of]).reshape(2, 2, 64, NB)

    for j in (2, 1, 3, 0):
        def one(row_y, _):
            row_step(row_y, (z + j) % 4)
        lax.fori_loop(0, 4, one, None)
        i = (z + j) % 4
        send(w_shard(0, 1 - k, i), sib.at[0, i], s0, (0, j), sibling)
    for j in (2, 1, 3, 0):
        i = (y + j) % 4
        send(w_shard(1, 1 - k, i), sib.at[1, i], s0, (1, j), sibling)
    for j in (2, 1, 3, 0):
        for f in range(2):
            i = (first[f] + j) % 4
            arrive(sib.at[f, i], s0, (f, j))
            acc[f, i] = w_shard(f, k, i)[...] + sib[f, i]
            up, down = first_peers[f][0], first_peers[f][2]
            if j == 2:
                send(acc.at[f, i, pl.ds(0, 2)], r1.at[f, 0], s1, (f, 0), up)
                send(acc.at[f, i, pl.ds(2, 2)], r1.at[f, 1], s1, (f, 1), down)
            if j == 1:
                send(acc.at[f, i, pl.ds(2, 2)], r2.at[f, 0, pl.ds(2, 2)], s2, (f, 0, 1), up)
            if j == 3:
                send(acc.at[f, i, pl.ds(0, 2)], r2.at[f, 1, pl.ds(0, 2)], s2, (f, 1, 0), down)
    @pl.when(gap == 3)
    def _():
        col_copy(0, 2, xp[2], 1).wait_recv()
        col_ref[0] = col_ref[0] + col_x[2, 0]
        col_copy(0, 0, xp[2], 1).start()

    @pl.when(gap == 1)
    def _():
        col_copy(1, 2, xp[0], 1).wait_recv()
        col_ref[1] = col_ref[1] + col_x[2, 1]
        col_copy(1, 1, xp[0], 1).start()

    invert(0)
    for f in range(2):
        up, down = first_peers[f][0], first_peers[f][2]
        i = (first[f] + 1) % 4
        arrive(r1.at[f, 0], s1, (f, 0))
        acc[f, i, 0:2] = acc[f, i, 0:2] + r1[f, 0]
        send(acc.at[f, i, pl.ds(0, 2)], r2.at[f, 0, pl.ds(0, 2)], s2, (f, 0, 0), up)
        i = (first[f] + 3) % 4
        arrive(r1.at[f, 1], s1, (f, 1))
        acc[f, i, 2:4] = acc[f, i, 2:4] + r1[f, 1]
        send(acc.at[f, i, pl.ds(2, 2)], r2.at[f, 1, pl.ds(2, 2)], s2, (f, 1, 1), down)

    invert(1)
    for d in range(3):
        arrive(m_x.at[d], sm, (1, d))
    m_b[...] = (m_a[r] + m_x[0] + (m_x[1] + m_x[2])).reshape(4, 32, 512)
    for d in range(3):
        send(m_b.at[(y + d + 1) % 4], m_y.at[d], sm, (2, d), yp[d])

    invert(2)
    for f in range(2):
        for side in range(2):
            for half in range(2):
                arrive(r2.at[f, side, pl.ds(2 * half, 2)], s2, (f, side, half))
        part[f] = acc[f, first[f]] + (r2[f, 0] + r2[f, 1])
        up, down = second_peers[f][0], second_peers[f][2]
        i = (second[f] + 2) % 4
        send(part.at[f, i, pl.ds(0, 32)], t1.at[f, 0], s3, (f, 0), up)
        send(part.at[f, i, pl.ds(32, 32)], t1.at[f, 1], s3, (f, 1), down)
        i = (second[f] + 1) % 4
        send(part.at[f, i, pl.ds(32, 32)], t2.at[f, 0, pl.ds(32, 32)], s4, (f, 0, 1), up)
        i = (second[f] + 3) % 4
        send(part.at[f, i, pl.ds(0, 32)], t2.at[f, 1, pl.ds(0, 32)], s4, (f, 1, 0), down)
    for d in range(3):
        arrive(m_y.at[d], sm, (2, d))
    m_c[...] = (m_b[y] + m_y[0] + (m_y[1] + m_y[2])).reshape(4, 8, 512)
    for d in range(3):
        send(m_c.at[(z + d + 1) % 4], m_z.at[d], sm, (3, d), zp[d])
    for f in range(2):
        up, down = second_peers[f][0], second_peers[f][2]
        i = (second[f] + 1) % 4
        arrive(t1.at[f, 0], s3, (f, 0))
        part[f, i, 0:32] = part[f, i, 0:32] + t1[f, 0]
        send(part.at[f, i, pl.ds(0, 32)], t2.at[f, 0, pl.ds(0, 32)], s4, (f, 0, 0), up)
        i = (second[f] + 3) % 4
        arrive(t1.at[f, 1], s3, (f, 1))
        part[f, i, 32:64] = part[f, i, 32:64] + t1[f, 1]
        send(part.at[f, i, pl.ds(32, 32)], t2.at[f, 1, pl.ds(32, 32)], s4, (f, 1, 1), down)
    @pl.when(r == own_col)
    def _():
        for slot in range(2):
            for b in range(2):
                col_copy(b, slot, sibling, 0).wait_recv()
        col_x[0] = col_ref[...] + (col_x[0] + col_x[1])
        for index, target in enumerate(targets):
            b, h = index // 2, index % 2

            @pl.when(target != c)
            def _():
                remote(col_x.at[0, b, h], col_p, sp.at[0, index], sp.at[1, 0], {"row": r, "col": target}).start()

            @pl.when(target == c)
            def _():
                col_p[...] = col_x[0, b, h]

    for d in range(3):
        arrive(m_z.at[d], sm, (3, d))
    m_f[k, r, y, z] = m_c[z] + m_z[0] + (m_z[1] + m_z[2])
    for d in range(3):
        send(m_f.at[k, r, y, z], m_f.at[k, r, y, z], sm, (4, d), zp[d])

    @pl.when(source != c)
    def _():
        remote(col_p, col_p, sp.at[0, 0], sp.at[1, 0], sibling).wait_recv()

    def piece(f, i1, i2, half=None, h=None):
        h = k if h is None else h
        ref = o_ref.at[i2, i1, h, f] if f == 0 else o_ref.at[i1, i2, h, f]
        return ref if half is None else ref.at[pl.ds(half * 32, 32)]

    link = h_ref[0, NB:]
    for f in range(2):
        for side in range(2):
            for half in range(2):
                arrive(t2.at[f, side, pl.ds(32 * half, 32)], s4, (f, side, half))
        rows = part[f, second[f]] + (t2[f, 0] + t2[f, 1]) - col_p[f * 64:f * 64 + 64, :]
        last = dot(rows[:, NB:], v[1])
        piece(f, first[f], second[f])[...] = jnp.concatenate([dot(rows[:, :NB] - dot(last, link), v[0]), last], 1)
        mine = piece(f, first[f], second[f])
        send(mine, mine, g1, (f, 0), second_peers[f][0])
        send(mine, mine, g1, (f, 1), second_peers[f][2])
        for s, to in ((0, 0), (1, 2)):
            send(mine, mine, g2, (f, 0, s), first_peers[f][to])
        send(mine, mine, gs, (f, 0, 0), sibling)

    zs = [(z + 4 - d) % 4 for d in (1, 2, 3)]
    for d in range(3):
        arrive(m_f.at[k, r, y, zs[d]], sm, (4, d))
    for d in range(3):
        send(m_f.at[k, r, y], m_f.at[k, r, y], sm, (5, d), yp[d])

    for f in range(2):
        i1, i2 = first[f], second[f]
        back, ahead = piece(f, i1, (i2 + 3) % 4), piece(f, i1, (i2 + 1) % 4)
        arrive(back, g1, (f, 0))
        half = piece(f, i1, (i2 + 3) % 4, 0)
        send(half, half, g1, (f, 2), second_peers[f][0])
        arrive(ahead, g1, (f, 1))
        half = piece(f, i1, (i2 + 1) % 4, 1)
        send(half, half, g1, (f, 3), second_peers[f][2])
        for e, ref in ((3, back), (1, ahead)):
            for s, to in ((0, 0), (1, 2)):
                send(ref, ref, g2, (f, e, s), first_peers[f][to])
            send(ref, ref, gs, (f, e, 0), sibling)

    ys = [(y + 4 - d) % 4 for d in (1, 2, 3)]
    for d in range(3):
        arrive(m_f.at[k, r, ys[d]], sm, (5, d))
    for d in range(3):
        @pl.when((r + d + 1) % 4 < 2)
        def _():
            remote(m_f.at[k, r], m_f.at[k, r], sm.at[0, 6, d], sm.at[1, 6, d], xp[d]).start()

    def relay(f, e):
        i1, i2 = first[f], (second[f] + e) % 4
        for s, near, to in ((0, 3, 0), (1, 1, 2)):
            got = piece(f, (i1 + near) % 4, i2)
            arrive(got, g2, (f, e, s))
            half = piece(f, (i1 + near) % 4, i2, s)
            send(half, half, g2, (f, e, 2 + s), first_peers[f][to])
            send(got, got, gs, (f, e, 1 + s), sibling)

    for f in range(2):
        relay(f, 0)
    for f in range(2):
        i1, i2 = first[f], (second[f] + 2) % 4
        for s in range(2):
            arrive(piece(f, i1, i2, s), g1, (f, 2 + s))
        far = piece(f, i1, i2)
        for s, to in ((0, 0), (1, 2)):
            send(far, far, g2, (f, 2, s), first_peers[f][to])
        send(far, far, gs, (f, 2, 0), sibling)
    for e in (3, 1):
        for f in range(2):
            relay(f, e)
    rs = [(r + 4 - d) % 4 for d in (1, 2, 3)]

    @pl.when(r < 2)
    def _():
        for d in range(3):
            arrive(m_f.at[k, rs[d]], sm, (6, d))
        remote(m_f.at[k], m_f.at[k], sm.at[0, 7, 0], sm.at[1, 7, 0], sibling).start()

    for f in range(2):
        relay(f, 2)
    @pl.when(r < 2)
    def _():
        arrive(m_f.at[1 - k], sm, (7, 0))
        m = m_f[...].reshape(1024, 512)
        l0, l1, v0, v1 = lower(h_ref[0, :NB]), lower(h_ref[1, NB:]), v[0], v[1]
        g1q = tdot(v1, m[NB:512])
        g1q0, g1q1 = g1q[:, :NB], g1q[:, NB:]
        k1 = lower(m[512:768, NB:]) - lower(g1q1)
        e1 = tdot(v1, dot(lower_half(tdot(l1, k1)), v1))
        e1 = lower_half(e1 + e1.T)
        g01 = dot(m[512:768, :NB] - dot(e1 + e1.T, link) - g1q0, v0)

        @pl.when(r == 1)
        def _():
            top_ref[:, :NB] = g01
            top_ref[:, NB:] = e1

        @pl.when(r == 0)
        def _():
            g0q0 = tdot(v0, m[:NB, :NB] - tdot(link, g1q0)) + tdot(g01, link)
            k0 = lower(m[768:, :NB]) - lower(g0q0)
            e0 = tdot(v0, dot(lower_half(tdot(l0, k0)), v0))
            top_ref[:, :NB] = lower_half(e0 + e0.T)
            top_ref[:, NB:] = jnp.zeros((NB, NB), jnp.float32)

    @pl.when(r >= 2)
    def _():
        top_ref[...] = jnp.zeros((NB, 512), jnp.float32)

    for e in (0, 3, 1, 2):
        for f in range(2):
            i1, i2 = first[f], (second[f] + e) % 4
            for s in range(2):
                arrive(piece(f, (i1 + 2) % 4, i2, s), g2, (f, e, 2 + s))
            far = piece(f, (i1 + 2) % 4, i2)
            send(far, far, gs, (f, e, 3), sibling)

    for e in range(4):
        for f in range(2):
            i1, i2 = first[f], (second[f] + e) % 4
            for s, near in enumerate((0, 3, 1, 2)):
                arrive(piece(f, (i1 + near) % 4, i2, None, 1 - k), gs, (f, e, s))
    for copy in sent:
        copy.wait_send()
    for d in range(3):
        @pl.when((r + d + 1) % 4 < 2)
        def _():
            remote(m_f.at[k, r], m_f.at[k, r], sm.at[0, 6, d], sm.at[1, 6, d], xp[d]).wait_send()

    @pl.when(r < 2)
    def _():
        remote(m_f.at[k], m_f.at[k], sm.at[0, 7, 0], sm.at[1, 7, 0], sibling).wait_send()

    @pl.when(r != own_col)
    def _():
        for which in range(2):
            col_copy(0, 2, sibling, which).wait_send()

    @pl.when(r == own_col)
    def _():
        for index, target in enumerate(targets):
            @pl.when(target != c)
            def _():
                remote(col_p, col_p, sp.at[0, index], sp.at[1, 0], sibling).wait_send()


def main_call(adjoint, p, q):
    f32, bf16 = jnp.float32, jnp.bfloat16
    vmem, dma = pltpu.VMEM, pltpu.SemaphoreType.DMA
    here = pl.BlockSpec(memory_space=pltpu.VMEM)
    there = pl.BlockSpec(memory_space=pl.ANY)
    o, top = pl.pallas_call(
        main_kernel,
        out_shape=(jax.ShapeDtypeStruct((4, 4, 2, 2, 64, 512), f32), jax.ShapeDtypeStruct((NB, 512), f32)),
        in_specs=[there, there, here],
        out_specs=(here, here),
        scratch_shapes=[
            vmem((16, NB, 512), f32), vmem((2, 2, NB, NB), f32), vmem((2, HEAD, NB), f32), vmem((2, NB, 512), bf16),
            vmem((2, NB, 512), bf16), vmem((NB, 512), f32), vmem((4, 4, 2, 2, 64, 512), f32), vmem((2, 2, 128, 512), f32),
            vmem((2, 4, 128, 512), f32),
            vmem((2, 4, 4, 64, 512), f32), vmem((2, 4, 4, 64, 512), f32), vmem((2, 2, 2, 64, 512), f32), vmem((2, 2, 4, 64, 512), f32),
            vmem((2, 4, 64, 512), f32), vmem((2, 2, 32, 512), f32), vmem((2, 2, 64, 512), f32), vmem((2, NB, NB), f32),
            vmem((3, 2, 2, 128, 512), f32), vmem((128, 512), f32), vmem((4, 128, 512), f32), vmem((4, 128, 512), f32),
            vmem((3, 128, 512), f32), vmem((4, 32, 512), f32), vmem((3, 32, 512), f32), vmem((4, 8, 512), f32), vmem((3, 8, 512), f32),
            vmem((2, 4, 4, 4, 8, 512), f32), dma((19,)),
            dma((2, 2, 4)), dma((2, 2, 2)), dma((2, 2, 2, 2)), dma((2, 2, 2)), dma((2, 2, 2, 2)), dma((2, 6)), dma((2, 4)),
            dma((2, 8, 3)), dma((2, 2, 4)), dma((2, 2, 4, 4)), dma((2, 2, 4, 4)),
        ],
        compiler_params=pltpu.CompilerParams(collective_id=2, has_side_effects=True, vmem_limit_bytes=62 << 20),
    )(adjoint, p, q)
    return o.reshape(ROWS, 512), top


def local(factor, adjoint):
    row_id = lax.axis_index("row")
    p, q = broadcast(factor)
    out, top = main_call(adjoint, p, q)
    rows = lax.broadcasted_iota(jnp.int32, out.shape, 0)
    return jnp.where((rows < NB) & (row_id < 2), jnp.pad(top, ((0, ROWS - NB), (0, 0))), out)


def solution(mesh):
    placed = (P("row", "col"), P("row", "col"))
    return jax.shard_map(local, mesh=mesh, in_specs=placed, out_specs=P("row", None), check_vma=False)
```

```python
import jax
import jax.numpy as jnp
from jax import lax
from jax.experimental import pallas as pl
from jax.experimental.pallas import tpu as pltpu
from jax.sharding import PartitionSpec as P

NB = 256
HIGHEST = lax.Precision.HIGHEST
HIGH = lax.Precision.HIGH


def dot(a, b, precision=HIGHEST):
    return lax.dot_general(a, b, (((1,), (0,)), ((), ())), precision=precision, preferred_element_type=jnp.float32)


def tdot(a, b, precision=HIGHEST):
    return lax.dot_general(a, b, (((0,), (0,)), ((), ())), precision=precision, preferred_element_type=jnp.float32)


def grid_ids(n):
    return lax.broadcasted_iota(jnp.int32, (n, n), 0), lax.broadcasted_iota(jnp.int32, (n, n), 1)


def lower(x):
    i, j = grid_ids(x.shape[0])
    return jnp.where(i >= j, x, 0.0)


def lower_half(x):
    i, j = grid_ids(x.shape[0])
    return jnp.where(i > j, x, jnp.where(i == j, 0.5 * x, 0.0))


MESH = pl.DeviceIdType.MESH
ROWS, HEAD, CHUNK = 4096, 512, 32
STEPS, LAG, AHEAD = 36, 5, 32
DEPTH = ((0, 3, 4, 3, 3, 4, 5, 4, 2, 3, 4, 3, 1, 2, 3, 2), (0, 3, 2, 1, 3, 4, 3, 2, 4, 5, 4, 3, 3, 4, 3, 2),
         (0, 3, 4, 3, 1, 2, 3, 2, 2, 3, 4, 3, 3, 4, 5, 4), (0, 1, 2, 3, 3, 2, 3, 4, 4, 3, 4, 5, 3, 2, 3, 4))
TREE_OF_LINK = ((2, 3, 3, 1, 2, 2, 3, 1, 2, 2, 2, 2, 9, 0, 0, 0), (3, 3, 3, 9, 2, 2, 3, 1, 0, 0, 3, 1, 0, 3, 3, 1),
                (0, 3, 1, 1, 9, 2, 2, 2, 0, 0, 0, 0, 0, 3, 1, 0), (1, 9, 1, 1, 2, 3, 1, 1, 2, 3, 1, 2, 0, 3, 1, 0))
LINKS = ((1, 0), (0, 1), (3, 0), (0, 3))


def place():
    r, c = lax.axis_index("row"), lax.axis_index("col")
    return r, c, c // 8, (c // 2) % 4, c % 2


def at(r, y, z, k):
    return {"row": r, "col": (y * 4 + z) * 2 + k}


def pick(index, table):
    value = jnp.int32(table[0])
    for i, entry in enumerate(table[1:], 1):
        value = jnp.where(index == i, jnp.int32(entry), value)
    return value


def remote(src, dst, send, recv, device):
    return pltpu.make_async_remote_copy(
        src_ref=src, dst_ref=dst, send_sem=send, recv_sem=recv, device_id=device, device_id_type=MESH
    )


def meet(devices):
    barrier = pltpu.get_barrier_semaphore()
    for device in devices:
        pl.semaphore_signal(barrier, inc=1, device_id=device, device_id_type=MESH)
    pl.semaphore_wait(barrier, len(devices))


def broadcast_kernel(f_ref, p_ref, q_ref, send, sib_send, recv, sib_recv, x_send, x_recv, h_send, h_recv, own):
    r, c, y, z, k = place()
    chip = y * 4 + z
    sibling = at(r, y, z, 1 - k)
    nexts = [at(r, (y + dy) % 4, (z + dz) % 4, k) for dy, dz in LINKS]
    xs = [at((r + d) % 4, y, z, k) for d in (1, 3, 2)]
    load = pltpu.make_async_copy(f_ref.at[:, pl.ds(0, NB)], p_ref.at[k, pl.ds(0, ROWS), :], own.at[0])

    @pl.when(chip == 0)
    def _():
        load.start()

    meet(nexts + [sibling] + xs)
    depth = [pick(chip, row) for row in DEPTH]
    tree = [pick(chip, row) for row in TREE_OF_LINK]
    is_root = chip == 0

    def first_row(s, t):
        u = jnp.where(s < AHEAD, s, s - 4)
        body = ((u % 8) * 2 + t // 2) * NB + (u // 8) * 64 + (t % 2) * CHUNK
        head = ROWS + ((s - AHEAD) * 4 + t) * CHUNK
        return pl.multiple_of(jnp.where((s >= AHEAD) & (s < AHEAD + 4), head, body), CHUNK)

    def pass_on(s, t, src, dst):
        to_links(s, t, src, dst)
        remote(src, dst, sib_send.at[s, t], sib_recv.at[s, t], sibling).start()

    def to_links(s, t, src, dst):
        for d in range(4):
            @pl.when(tree[d] == t)
            def _():
                remote(src, dst, send.at[d, s], recv.at[s, t], nexts[d]).start()

    @pl.when(is_root)
    def _():
        for head in range(2):
            rows = p_ref.at[k, pl.ds(ROWS + head * NB, NB), :]
            block = f_ref.at[pl.ds(0, NB), pl.ds(0, NB)]

            @pl.when(r == head)
            def _():
                pltpu.make_async_copy(block, rows, own.at[1]).start()
                for i, device in enumerate(xs):
                    remote(block, rows, h_send.at[i], h_recv.at[head], device).start()

        def from_own(s, _):
            for t in range(4):
                rows = p_ref.at[k, pl.ds(first_row(s, t), CHUNK), :]
                pass_on(s, t, rows, rows)

        load.wait()
        lax.fori_loop(0, AHEAD, from_own, None)
        for head in range(2):
            rows = p_ref.at[k, pl.ds(ROWS + head * NB, NB), :]

            @pl.when(r == head)
            def _():
                pltpu.make_async_copy(rows, rows, own.at[1]).wait()
                for i, device in enumerate(xs):
                    remote(rows, rows, h_send.at[i], h_recv.at[head], device).wait_send()

            @pl.when(r != head)
            def _():
                remote(rows, rows, h_send.at[0], h_recv.at[head], xs[0]).wait_recv()

        lax.fori_loop(AHEAD, STEPS, from_own, None)

    def forward(n, _):
        for t in range(4):
            s = n - LAG * (depth[t] - 1)

            @pl.when((s >= 0) & (s < STEPS))
            def _():
                rows = p_ref.at[k, pl.ds(first_row(s, t), CHUNK), :]
                remote(rows, rows, sib_send.at[s, t], recv.at[s, t], sibling).wait_recv()
                pass_on(s, t, rows, rows)

    m = c // 4
    stops = [8 * j + 8 + (4 if 8 * j >= AHEAD else 0) + LAG * 4 for j in range(4)]
    for j in range(4):
        @pl.when(jnp.logical_not(is_root))
        def _():
            lax.fori_loop(stops[j - 1] if j else 0, stops[j], forward, None)

        @pl.when(r == c % 4)
        def _():
            for b in range(2):
                row = pl.multiple_of((m + 8 * b) * NB + j * 64, 64)
                s = (j * 8 + 4 * b + m // 2) + (4 if 8 * j >= AHEAD else 0)
                for half in range(2):
                    t = (m % 2) * 2 + half
                    got = p_ref.at[1 - k, pl.ds(row + half * CHUNK, CHUNK), :]
                    remote(got, got, sib_send.at[s, t], sib_recv.at[s, t], sibling).wait_recv()
                src = p_ref.at[:, pl.ds(row, 64), :]
                dst = q_ref.at[:, pl.ds(b * NB + j * 64, 64), :]
                pltpu.make_async_copy(src, dst, own.at[2 + j * 2 + b]).start()
                for i, device in enumerate(xs):
                    remote(src, dst, x_send.at[j, b, i], x_recv.at[j, b], device).start()

    @pl.when(jnp.logical_not(is_root))
    def _():
        lax.fori_loop(stops[3], STEPS + LAG * 4, forward, None)

    def finish(s, _):
        for t in range(4):
            row = first_row(s, t)
            mine = p_ref.at[k, pl.ds(row, CHUNK), :]
            other = p_ref.at[1 - k, pl.ds(row, CHUNK), :]
            remote(mine, mine, sib_send.at[s, t], sib_recv.at[s, t], sibling).wait_send()
            u = jnp.where(s < AHEAD, s, s - 4)
            block = (u % 8) * 2 + t // 2
            early = (r == c % 4) & ((s < AHEAD) | (s >= AHEAD + 4)) & (block % 8 == m)

            @pl.when(jnp.logical_not(early))
            def _():
                remote(other, other, sib_send.at[s, t], sib_recv.at[s, t], sibling).wait_recv()
        for d in range(4):
            @pl.when(tree[d] < 4)
            def _():
                rows = p_ref.at[k, pl.ds(0, CHUNK), :]
                remote(rows, rows, send.at[d, s], recv.at[s, 0], nexts[d]).wait_send()

    lax.fori_loop(0, STEPS, finish, None)
    for j in range(4):
        for b in range(2):
            src = p_ref.at[:, pl.ds(0, 64), :]
            dst = q_ref.at[:, pl.ds(b * NB + j * 64, 64), :]

            @pl.when(r == c % 4)
            def _():
                pltpu.make_async_copy(src, dst, own.at[2 + j * 2 + b]).wait()
                for i, device in enumerate(xs):
                    remote(src, dst, x_send.at[j, b, i], x_recv.at[j, b], device).wait_send()

            @pl.when(r != c % 4)
            def _():
                remote(src, dst, x_send.at[j, b, 0], x_recv.at[j, b], xs[0]).wait_recv()


def broadcast(factor):
    dma = pltpu.SemaphoreType.DMA
    return pl.pallas_call(
        broadcast_kernel,
        out_shape=(jax.ShapeDtypeStruct((2, ROWS + HEAD, NB), jnp.float32), jax.ShapeDtypeStruct((2, 512, NB), jnp.float32)),
        in_specs=[pl.BlockSpec(memory_space=pltpu.HBM)],
        out_specs=(pl.BlockSpec(memory_space=pltpu.VMEM),) * 2,
        scratch_shapes=[dma((4, STEPS)), dma((STEPS, 4)), dma((STEPS, 4)), dma((STEPS, 4)), dma((4, 2, 3)), dma((4, 2)),
                        dma((3,)), dma((2,)), dma((10,))],
        compiler_params=pltpu.CompilerParams(collective_id=1, has_side_effects=True, vmem_limit_bytes=60 << 20),
    )(factor)


def split(x):
    high = x.astype(jnp.bfloat16)
    return high, (x - high.astype(jnp.float32)).astype(jnp.bfloat16)


def dot3(a, b, dims):
    def one(x, w):
        return lax.dot_general(x, w, (dims, ((), ())), preferred_element_type=jnp.float32)
    return one(a[0], b[0]) + (one(a[0], b[1]) + one(a[1], b[0]))


def inverse_first(mats):
    i, j = grid_ids(NB)
    d = [jnp.where(i == j, 1.0 / jnp.where(i == j, m, 1.0), 0.0) for m in mats]
    return inverse_level(mats, d, 1)


def inverse_level(mats, found, size):
    i, j = grid_ids(NB)
    corner = (i // (2 * size) == j // (2 * size)) & (i // size > j // size)
    inner = [dot(jnp.where(corner, m, 0.0), x) for m, x in zip(mats, found)]
    return [x - dot(x, y) for x, y in zip(found, inner)]


def main_kernel(a_hbm, p_hbm, q_ref, o_ref, top_ref, a_ref, p_ref, h_ref, qh, ql, row_acc, w_ref, col_ref, m_ref, acc, sib, r1, r2, part, t1, t2, v, col_x, col_p, m_a, m_s, m_x, m_b,
                  m_y, m_c, m_z, m_f, sl, s0, s1, s2, s3, s4, sc, sp, sm, g1, g2, gs):
    r, c, y, z, k = place()
    sibling = at(r, y, z, 1 - k)
    xp = [at((r + d) % 4, y, z, k) for d in (1, 2, 3)]
    yp = [at(r, (y + d) % 4, z, k) for d in (1, 2, 3)]
    zp = [at(r, y, (z + d) % 4, k) for d in (1, 2, 3)]
    own_col = c % 4
    m_id = c // 4
    chip = y * 4 + z
    source = (4 * chip + r) % 32
    barrier = pltpu.get_barrier_semaphore()
    for device in xp + yp + zp + [sibling]:
        pl.semaphore_signal(barrier, inc=1, device_id=device, device_id_type=MESH)
    others = jnp.int32(0)
    targets = [2 * (m_id + 8 * b) + h for b in range(2) for h in range(2)]
    for target in targets:
        others += jnp.where((r == own_col) & (target != c), 1, 0).astype(jnp.int32)

    @pl.when(source != c)
    def _():
        pl.semaphore_signal(barrier, inc=1, device_id={"row": r, "col": source}, device_id_type=MESH)

    def load_a(a):
        rows = pl.ds(pl.multiple_of(a * NB, NB), NB)
        return pltpu.make_async_copy(a_hbm.at[rows], a_ref.at[a], sl.at[a])

    def load_p(a):
        rows = pl.ds(pl.multiple_of(a * NB, NB), NB)
        return pltpu.make_async_copy(p_hbm.at[:, rows], p_ref.at[a % 2], sl.at[16 + a % 2])

    load_h = pltpu.make_async_copy(p_hbm.at[:, pl.ds(ROWS, HEAD)], h_ref, sl.at[18])
    load_p(0).start()
    for a in range(16):
        load_a(a).start()
    load_h.start()
    i_ids, j_ids = grid_ids(NB)
    col_ref[...] = jnp.zeros_like(col_ref)
    m_ref[...] = jnp.zeros_like(m_ref)
    for b in range(2):
        for side in range(2):
            qh[b, :, side * NB:(side + 1) * NB], ql[b, :, side * NB:(side + 1) * NB] = split(q_ref[side, b * NB:(b + 1) * NB, :])

    def tile_of(a, b):
        column = 32 * b + c
        tile = a_ref[a, :, b * NB:(b + 1) * NB]
        return split(jnp.where((4 * a + r > column) | (i_ids >= j_ids), tile, 0.0))

    def column_step(a, _):
        @pl.when(a < 15)
        def _():
            load_p(a + 1).start()
        load_a(a).wait()
        load_p(a).wait()
        panel = split(jnp.concatenate([p_ref[a % 2, 0], p_ref[a % 2, 1]], 1))
        for b in range(2):
            @pl.when((4 * a + r >= 32 * b + c) & (4 * a + r >= 2))
            def _():
                col_ref[b] += dot3(tile_of(a, b), panel, ((0,), (0,))).reshape(2, 128, 512)

    lax.fori_loop(0, 16, column_step, None)
    for hr, hc, lo, side in ((0, 0, 2, 0), (1, 0, 0, 0), (1, 1, 0, NB)):
        @pl.when((r == hr) & (c == hc))
        def _():
            m_ref[1, lo:lo + 2, :, side:side + NB] = a_ref[0, :, :NB].reshape(2, 128, NB)
    for side in range(2):
        @pl.when(c == side)
        def _():
            m_ref[0, 2 * side:2 * side + 2] = col_ref[0]

    @pl.when(c < 2)
    def _():
        col_ref[0] = jnp.zeros((2, 128, 512), jnp.float32)

    gram = jnp.zeros((512, 512), jnp.float32)
    for b in range(2):
        gram += dot3(split(col_ref[b].reshape(NB, 512)), (qh[b], ql[b]), ((0,), (0,)))
    m_ref[0] += (-gram - gram.T).reshape(4, 128, 512)
    load_h.wait()
    pl.semaphore_wait(barrier, 10 + others)

    sent = []

    def send(src, dst, sems, index, device):
        copy = remote(src, dst, sems.at[(0, *index)], sems.at[(1, *index)], device)
        copy.start()
        sent.append(copy)

    def arrive(dst, sems, index):
        remote(dst, dst, sems.at[(0, *index)], sems.at[(1, *index)], sibling).wait_recv()

    def invert(stage):
        low = [lower(h_ref[0, :NB]), lower(h_ref[1, NB:])]
        found = inverse_first(low) if stage == 0 else [v[0], v[1]]
        for size in ((2, 4), (8, 16, 32), (64, 128))[stage]:
            found = inverse_level(low, found, size)
        v[0], v[1] = found

    first = [z, y]
    second = [y, z]
    first_peers, second_peers = [zp, yp], [yp, zp]

    def w_shard(f, h, i):
        return w_ref.at[:, i, h, 0] if f == 0 else w_ref.at[i, :, h, 1]

    send(m_ref.at[1 - k], m_s, sm, (0, 0), sibling)
    arrive(m_s, sm, (0, 0))
    m_a[...] = m_ref[k] + m_s[...]
    for d in range(3):
        send(m_a.at[(r + d + 1) % 4], m_x.at[d], sm, (1, d), xp[d])

    gap = (own_col - r + 4) % 4

    def col_copy(b, slot, device, which):
        return remote(col_ref.at[b], col_x.at[slot, b], sc.at[0, which], sc.at[1, 2 * slot + b], device)

    @pl.when(gap == 2)
    def _():
        col_copy(0, 2, xp[2], 0).start()
        col_copy(1, 2, xp[0], 1).start()

    @pl.when(gap == 3)
    def _():
        col_copy(1, 0, xp[2], 0).start()

    @pl.when(gap == 1)
    def _():
        col_copy(0, 1, xp[0], 0).start()

    def row_step(row_y, row_z):
        a = 4 * row_y + row_z
        row_acc[...] = jnp.zeros_like(row_acc)
        for b in range(2):
            column = 32 * b + c

            @pl.when((4 * a + r >= column) & (column >= 2))
            def _():
                row_acc[...] += dot3(tile_of(a, b), (qh[b], ql[b]), ((1,), (0,)))
        for side in range(2):
            part_of = slice(side * NB, (side + 1) * NB)
            own = jnp.where(c == side, a_ref[a, :, :NB], 0.0)
            w_ref[row_y, row_z, :, :, :, part_of] = (own - row_acc[:, part_of]).reshape(2, 2, 64, NB)

    for j in (2, 1, 3, 0):
        def one(row_y, _):
            row_step(row_y, (z + j) % 4)
        lax.fori_loop(0, 4, one, None)
        i = (z + j) % 4
        send(w_shard(0, 1 - k, i), sib.at[0, i], s0, (0, j), sibling)
    for j in (2, 1, 3, 0):
        i = (y + j) % 4
        send(w_shard(1, 1 - k, i), sib.at[1, i], s0, (1, j), sibling)
    for j in (2, 1, 3, 0):
        for f in range(2):
            i = (first[f] + j) % 4
            arrive(sib.at[f, i], s0, (f, j))
            acc[f, i] = w_shard(f, k, i)[...] + sib[f, i]
            up, down = first_peers[f][0], first_peers[f][2]
            if j == 2:
                send(acc.at[f, i, pl.ds(0, 2)], r1.at[f, 0], s1, (f, 0), up)
                send(acc.at[f, i, pl.ds(2, 2)], r1.at[f, 1], s1, (f, 1), down)
            if j == 1:
                send(acc.at[f, i, pl.ds(2, 2)], r2.at[f, 0, pl.ds(2, 2)], s2, (f, 0, 1), up)
            if j == 3:
                send(acc.at[f, i, pl.ds(0, 2)], r2.at[f, 1, pl.ds(0, 2)], s2, (f, 1, 0), down)
    @pl.when(gap == 3)
    def _():
        col_copy(0, 2, xp[2], 1).wait_recv()
        col_ref[0] = col_ref[0] + col_x[2, 0]
        col_copy(0, 0, xp[2], 1).start()

    @pl.when(gap == 1)
    def _():
        col_copy(1, 2, xp[0], 1).wait_recv()
        col_ref[1] = col_ref[1] + col_x[2, 1]
        col_copy(1, 1, xp[0], 1).start()

    invert(0)
    for f in range(2):
        up, down = first_peers[f][0], first_peers[f][2]
        i = (first[f] + 1) % 4
        arrive(r1.at[f, 0], s1, (f, 0))
        acc[f, i, 0:2] = acc[f, i, 0:2] + r1[f, 0]
        send(acc.at[f, i, pl.ds(0, 2)], r2.at[f, 0, pl.ds(0, 2)], s2, (f, 0, 0), up)
        i = (first[f] + 3) % 4
        arrive(r1.at[f, 1], s1, (f, 1))
        acc[f, i, 2:4] = acc[f, i, 2:4] + r1[f, 1]
        send(acc.at[f, i, pl.ds(2, 2)], r2.at[f, 1, pl.ds(2, 2)], s2, (f, 1, 1), down)

    invert(1)
    for d in range(3):
        arrive(m_x.at[d], sm, (1, d))
    m_b[...] = (m_a[r] + m_x[0] + (m_x[1] + m_x[2])).reshape(4, 32, 512)
    for d in range(3):
        send(m_b.at[(y + d + 1) % 4], m_y.at[d], sm, (2, d), yp[d])

    invert(2)
    for f in range(2):
        for side in range(2):
            for half in range(2):
                arrive(r2.at[f, side, pl.ds(2 * half, 2)], s2, (f, side, half))
        part[f] = acc[f, first[f]] + (r2[f, 0] + r2[f, 1])
        up, down = second_peers[f][0], second_peers[f][2]
        i = (second[f] + 2) % 4
        send(part.at[f, i, pl.ds(0, 32)], t1.at[f, 0], s3, (f, 0), up)
        send(part.at[f, i, pl.ds(32, 32)], t1.at[f, 1], s3, (f, 1), down)
        i = (second[f] + 1) % 4
        send(part.at[f, i, pl.ds(32, 32)], t2.at[f, 0, pl.ds(32, 32)], s4, (f, 0, 1), up)
        i = (second[f] + 3) % 4
        send(part.at[f, i, pl.ds(0, 32)], t2.at[f, 1, pl.ds(0, 32)], s4, (f, 1, 0), down)
    for d in range(3):
        arrive(m_y.at[d], sm, (2, d))
    m_c[...] = (m_b[y] + m_y[0] + (m_y[1] + m_y[2])).reshape(4, 8, 512)
    for d in range(3):
        send(m_c.at[(z + d + 1) % 4], m_z.at[d], sm, (3, d), zp[d])
    for f in range(2):
        up, down = second_peers[f][0], second_peers[f][2]
        i = (second[f] + 1) % 4
        arrive(t1.at[f, 0], s3, (f, 0))
        part[f, i, 0:32] = part[f, i, 0:32] + t1[f, 0]
        send(part.at[f, i, pl.ds(0, 32)], t2.at[f, 0, pl.ds(0, 32)], s4, (f, 0, 0), up)
        i = (second[f] + 3) % 4
        arrive(t1.at[f, 1], s3, (f, 1))
        part[f, i, 32:64] = part[f, i, 32:64] + t1[f, 1]
        send(part.at[f, i, pl.ds(32, 32)], t2.at[f, 1, pl.ds(32, 32)], s4, (f, 1, 1), down)
    @pl.when(r == own_col)
    def _():
        for slot in range(2):
            for b in range(2):
                col_copy(b, slot, sibling, 0).wait_recv()
        col_x[0] = col_ref[...] + (col_x[0] + col_x[1])
        for index, target in enumerate(targets):
            b, h = index // 2, index % 2

            @pl.when(target != c)
            def _():
                remote(col_x.at[0, b, h], col_p, sp.at[0, index], sp.at[1, 0], {"row": r, "col": target}).start()

            @pl.when(target == c)
            def _():
                col_p[...] = col_x[0, b, h]

    for d in range(3):
        arrive(m_z.at[d], sm, (3, d))
    m_f[k, r, y, z] = m_c[z] + m_z[0] + (m_z[1] + m_z[2])
    for d in range(3):
        send(m_f.at[k, r, y, z], m_f.at[k, r, y, z], sm, (4, d), zp[d])

    @pl.when(source != c)
    def _():
        remote(col_p, col_p, sp.at[0, 0], sp.at[1, 0], sibling).wait_recv()

    def piece(f, i1, i2, half=None, h=None):
        h = k if h is None else h
        ref = o_ref.at[i2, i1, h, f] if f == 0 else o_ref.at[i1, i2, h, f]
        return ref if half is None else ref.at[pl.ds(half * 32, 32)]

    link = h_ref[0, NB:]
    for f in range(2):
        for side in range(2):
            for half in range(2):
                arrive(t2.at[f, side, pl.ds(32 * half, 32)], s4, (f, side, half))
        rows = part[f, second[f]] + (t2[f, 0] + t2[f, 1]) - col_p[f * 64:f * 64 + 64, :]
        last = dot(rows[:, NB:], v[1])
        piece(f, first[f], second[f])[...] = jnp.concatenate([dot(rows[:, :NB] - dot(last, link), v[0]), last], 1)
        mine = piece(f, first[f], second[f])
        send(mine, mine, g1, (f, 0), second_peers[f][0])
        send(mine, mine, g1, (f, 1), second_peers[f][2])
        for s, to in ((0, 0), (1, 2)):
            send(mine, mine, g2, (f, 0, s), first_peers[f][to])
        send(mine, mine, gs, (f, 0, 0), sibling)

    zs = [(z + 4 - d) % 4 for d in (1, 2, 3)]
    for d in range(3):
        arrive(m_f.at[k, r, y, zs[d]], sm, (4, d))
    for d in range(3):
        send(m_f.at[k, r, y], m_f.at[k, r, y], sm, (5, d), yp[d])

    for f in range(2):
        i1, i2 = first[f], second[f]
        back, ahead = piece(f, i1, (i2 + 3) % 4), piece(f, i1, (i2 + 1) % 4)
        arrive(back, g1, (f, 0))
        half = piece(f, i1, (i2 + 3) % 4, 0)
        send(half, half, g1, (f, 2), second_peers[f][0])
        arrive(ahead, g1, (f, 1))
        half = piece(f, i1, (i2 + 1) % 4, 1)
        send(half, half, g1, (f, 3), second_peers[f][2])
        for e, ref in ((3, back), (1, ahead)):
            for s, to in ((0, 0), (1, 2)):
                send(ref, ref, g2, (f, e, s), first_peers[f][to])
            send(ref, ref, gs, (f, e, 0), sibling)

    ys = [(y + 4 - d) % 4 for d in (1, 2, 3)]
    for d in range(3):
        arrive(m_f.at[k, r, ys[d]], sm, (5, d))
    for d in range(3):
        @pl.when((r + d + 1) % 4 < 2)
        def _():
            remote(m_f.at[k, r], m_f.at[k, r], sm.at[0, 6, d], sm.at[1, 6, d], xp[d]).start()

    def relay(f, e):
        i1, i2 = first[f], (second[f] + e) % 4
        for s, near, to in ((0, 3, 0), (1, 1, 2)):
            got = piece(f, (i1 + near) % 4, i2)
            arrive(got, g2, (f, e, s))
            half = piece(f, (i1 + near) % 4, i2, s)
            send(half, half, g2, (f, e, 2 + s), first_peers[f][to])
            send(got, got, gs, (f, e, 1 + s), sibling)

    for f in range(2):
        relay(f, 0)
    for f in range(2):
        i1, i2 = first[f], (second[f] + 2) % 4
        for s in range(2):
            arrive(piece(f, i1, i2, s), g1, (f, 2 + s))
        far = piece(f, i1, i2)
        for s, to in ((0, 0), (1, 2)):
            send(far, far, g2, (f, 2, s), first_peers[f][to])
        send(far, far, gs, (f, 2, 0), sibling)
    for e in (3, 1):
        for f in range(2):
            relay(f, e)
    rs = [(r + 4 - d) % 4 for d in (1, 2, 3)]

    @pl.when(r < 2)
    def _():
        for d in range(3):
            arrive(m_f.at[k, rs[d]], sm, (6, d))
        remote(m_f.at[k], m_f.at[k], sm.at[0, 7, 0], sm.at[1, 7, 0], sibling).start()

    for f in range(2):
        relay(f, 2)
    @pl.when(r < 2)
    def _():
        arrive(m_f.at[1 - k], sm, (7, 0))
        m = m_f[...].reshape(1024, 512)
        l0, l1, v0, v1 = lower(h_ref[0, :NB]), lower(h_ref[1, NB:]), v[0], v[1]
        g1q = tdot(v1, m[NB:512])
        g1q0, g1q1 = g1q[:, :NB], g1q[:, NB:]
        k1 = lower(m[512:768, NB:]) - lower(g1q1)
        e1 = tdot(v1, dot(lower_half(tdot(l1, k1)), v1))
        e1 = lower_half(e1 + e1.T)
        g01 = dot(m[512:768, :NB] - dot(e1 + e1.T, link) - g1q0, v0)

        @pl.when(r == 1)
        def _():
            top_ref[:, :NB] = g01
            top_ref[:, NB:] = e1

        @pl.when(r == 0)
        def _():
            g0q0 = tdot(v0, m[:NB, :NB] - tdot(link, g1q0)) + tdot(g01, link)
            k0 = lower(m[768:, :NB]) - lower(g0q0)
            e0 = tdot(v0, dot(lower_half(tdot(l0, k0)), v0))
            top_ref[:, :NB] = lower_half(e0 + e0.T)
            top_ref[:, NB:] = jnp.zeros((NB, NB), jnp.float32)

    @pl.when(r >= 2)
    def _():
        top_ref[...] = jnp.zeros((NB, 512), jnp.float32)

    for e in (0, 3, 1, 2):
        for f in range(2):
            i1, i2 = first[f], (second[f] + e) % 4
            for s in range(2):
                arrive(piece(f, (i1 + 2) % 4, i2, s), g2, (f, e, 2 + s))
            far = piece(f, (i1 + 2) % 4, i2)
            send(far, far, gs, (f, e, 3), sibling)

    for e in range(4):
        for f in range(2):
            i1, i2 = first[f], (second[f] + e) % 4
            for s, near in enumerate((0, 3, 1, 2)):
                arrive(piece(f, (i1 + near) % 4, i2, None, 1 - k), gs, (f, e, s))
    for copy in sent:
        copy.wait_send()
    for d in range(3):
        @pl.when((r + d + 1) % 4 < 2)
        def _():
            remote(m_f.at[k, r], m_f.at[k, r], sm.at[0, 6, d], sm.at[1, 6, d], xp[d]).wait_send()

    @pl.when(r < 2)
    def _():
        remote(m_f.at[k], m_f.at[k], sm.at[0, 7, 0], sm.at[1, 7, 0], sibling).wait_send()

    @pl.when(r != own_col)
    def _():
        for which in range(2):
            col_copy(0, 2, sibling, which).wait_send()

    @pl.when(r == own_col)
    def _():
        for index, target in enumerate(targets):
            @pl.when(target != c)
            def _():
                remote(col_p, col_p, sp.at[0, index], sp.at[1, 0], sibling).wait_send()


def main_call(adjoint, p, q):
    f32, bf16 = jnp.float32, jnp.bfloat16
    vmem, dma = pltpu.VMEM, pltpu.SemaphoreType.DMA
    here = pl.BlockSpec(memory_space=pltpu.VMEM)
    there = pl.BlockSpec(memory_space=pl.ANY)
    o, top = pl.pallas_call(
        main_kernel,
        out_shape=(jax.ShapeDtypeStruct((4, 4, 2, 2, 64, 512), f32), jax.ShapeDtypeStruct((NB, 512), f32)),
        in_specs=[there, there, here],
        out_specs=(here, here),
        scratch_shapes=[
            vmem((16, NB, 512), f32), vmem((2, 2, NB, NB), f32), vmem((2, HEAD, NB), f32), vmem((2, NB, 512), bf16),
            vmem((2, NB, 512), bf16), vmem((NB, 512), f32), vmem((4, 4, 2, 2, 64, 512), f32), vmem((2, 2, 128, 512), f32),
            vmem((2, 4, 128, 512), f32),
            vmem((2, 4, 4, 64, 512), f32), vmem((2, 4, 4, 64, 512), f32), vmem((2, 2, 2, 64, 512), f32), vmem((2, 2, 4, 64, 512), f32),
            vmem((2, 4, 64, 512), f32), vmem((2, 2, 32, 512), f32), vmem((2, 2, 64, 512), f32), vmem((2, NB, NB), f32),
            vmem((3, 2, 2, 128, 512), f32), vmem((128, 512), f32), vmem((4, 128, 512), f32), vmem((4, 128, 512), f32),
            vmem((3, 128, 512), f32), vmem((4, 32, 512), f32), vmem((3, 32, 512), f32), vmem((4, 8, 512), f32), vmem((3, 8, 512), f32),
            vmem((2, 4, 4, 4, 8, 512), f32), dma((19,)),
            dma((2, 2, 4)), dma((2, 2, 2)), dma((2, 2, 2, 2)), dma((2, 2, 2)), dma((2, 2, 2, 2)), dma((2, 6)), dma((2, 4)),
            dma((2, 8, 3)), dma((2, 2, 4)), dma((2, 2, 4, 4)), dma((2, 2, 4, 4)),
        ],
        compiler_params=pltpu.CompilerParams(collective_id=2, has_side_effects=True, vmem_limit_bytes=62 << 20),
    )(adjoint, p, q)
    return o.reshape(ROWS, 512), top


def local(factor, adjoint):
    row_id = lax.axis_index("row")
    p, q = broadcast(factor)
    out, top = main_call(adjoint, p, q)
    rows = lax.broadcasted_iota(jnp.int32, out.shape, 0)
    return jnp.where((rows < NB) & (row_id < 2), jnp.pad(top, ((0, ROWS - NB), (0, 0))), out)


def solution(mesh):
    placed = (P("row", "col"), P("row", "col"))
    return jax.shard_map(local, mesh=mesh, in_specs=placed, out_specs=P("row", None), check_vma=False)
```
